768 devices in a mesh: ctx: 32 (over y_hi, x, core), tp: 24 (over y_lo, z).
Axes of the slice: x: 4, y: 8 (y_hi: 4, y_lo: 2; y = y_hi * 2 + y_lo), z: 12, core: 2. Of those that a mesh axis runs over, the one named last changes fastest.
Arguments:
- tokens: bfloat16 [18432, 4096], P(('ctx', 'tp')), may hold values from -6 to 6
- proj_weight: bfloat16 [4096, 3, 3072], P(None, None, 'tp'), may hold values from -0.09375 to 0.09375
- feat_taps: float32 [3, 3, 3072], P(None, None, 'tp'), may hold values from -2.5 to 2.5
- inner_taps: float32 [7, 3072], P(None, 'tp'), may hold values from -2.5 to 2.5
- grad_out: bfloat16 [18432, 3072], P('ctx', 'tp'), may hold values from -6 to 6
Outputs:
- gated: bfloat16 [18432, 3072], P('ctx', 'tp')
- grad_tokens: bfloat16 [18432, 4096], P(('ctx', 'tp'))
The draws below stay inside these ranges and needn't reach their ends.
All inputs are finite; a program needn't handle non-finite values.
Results may differ from the reference program's by a relative error of at most 0.025.
Values may be sent and summed in bfloat16 or wider, within the bound.
No kernel may reach another device: no remote copies, remote signals or barrier semaphores. Data moves between devices by JAX's collectives and lax.ppermute only.
A program may use at most 32 MiB of HBM per device.

```python
import jax
import jax.numpy as jnp
from jax import lax

D = 4096
FTAPS = 3
ITAPS = 7
CH = 3072
SEQ = 18432
N_TP = 24


def block_scale(key, shape, cuts, low, top_value):
    gain = 1.0
    for position, shards_of in cuts:
        steps = jax.random.uniform(jax.random.fold_in(jax.random.fold_in(key, 6), position), (shards_of,), jnp.float32, low / len(cuts), top_value / len(cuts))
        gain = gain * jnp.repeat(jnp.exp(steps), shape[position] // shards_of).reshape((-1,) + (1,) * (len(shape) - 1 - position))
    return gain


def noise(stream_key, dims, deviation, reach, pieces=(), dtype=jnp.bfloat16):
    factor_of = block_scale(stream_key, dims, pieces, -0.22, 0.18) if pieces else 1.0
    drawn = jax.random.normal(stream_key, dims, jnp.float32) * deviation * factor_of
    return jnp.minimum(jnp.maximum(drawn, -reach), reach).astype(dtype)


def setup_inputs(seed: int = 0) -> dict:
    keys = jax.random.split(jax.random.key(seed), 6)
    return {
        "tokens": noise(keys[0], (SEQ, D), 1.0, 6.0, ((0, 768),)),
        "proj_weight": noise(keys[1], (D, 3, CH), D ** -0.5, 0.09375, ((2, 24),)),
        "feat_taps": noise(keys[2], (3, FTAPS, CH), 0.6, 2.5, ((2, 24),), jnp.float32),
        "inner_taps": noise(keys[3], (ITAPS, CH), 0.4, 2.5, ((1, 24),), jnp.float32),
        "grad_out": noise(keys[4], (SEQ, CH), 1.0, 6.0, ((0, 32), (1, 24))),
    }


def causal_taps(series, kernel):
    taps = kernel.shape[0]
    length = series.shape[0] - (taps - 1)
    summed = kernel[0] * series[taps - 1:taps - 1 + length]
    for offset in range(1, taps):
        summed = summed + kernel[offset] * series[taps - 1 - offset:taps - 1 - offset + length]
    return summed


def anti_taps(series, kernel):
    taps = kernel.shape[0]
    length = series.shape[0] - (taps - 1)
    summed = kernel[0] * series[0:length]
    for offset in range(1, taps):
        summed = summed + kernel[offset] * series[offset:offset + length]
    return summed


def featurize(window, feat_taps, inner_taps):
    query_feat = causal_taps(window[6:, 0], feat_taps[0])
    key_feat = causal_taps(window[:, 1], feat_taps[1])
    value_feat = causal_taps(window[:, 2], feat_taps[2])
    inner_conv = causal_taps(key_feat * value_feat, inner_taps)
    return query_feat, key_feat, value_feat, inner_conv


def reference(tokens, proj_weight, feat_taps, inner_taps, grad_out):
    flat_weight = proj_weight.reshape(D, 3 * CH)
    projected = jnp.dot(tokens, flat_weight, preferred_element_type=jnp.float32).astype(jnp.bfloat16)
    projected = projected.reshape(SEQ, 3, CH).astype(jnp.float32)
    window = jnp.concatenate([jnp.zeros((8, 3, CH), jnp.float32), projected], axis=0)
    query_feat, key_feat, value_feat, inner_conv = featurize(window, feat_taps, inner_taps)
    gated = (query_feat * inner_conv).astype(jnp.bfloat16)
    grad_f = grad_out.astype(jnp.float32)
    grad_query = grad_f * inner_conv
    grad_inner = grad_f * query_feat
    grad_mix = anti_taps(jnp.concatenate([grad_inner, jnp.zeros((6, CH), jnp.float32)], axis=0), inner_taps)
    grad_key = grad_mix * value_feat[6:]
    grad_value = grad_mix * key_feat[6:]
    pad_two = jnp.zeros((2, CH), jnp.float32)
    grad_proj = jnp.stack([
        anti_taps(jnp.concatenate([grad_query, pad_two], axis=0), feat_taps[0]),
        anti_taps(jnp.concatenate([grad_key, pad_two], axis=0), feat_taps[1]),
        anti_taps(jnp.concatenate([grad_value, pad_two], axis=0), feat_taps[2])], axis=1)
    grad_proj = grad_proj.astype(jnp.bfloat16)
    group = CH // N_TP
    total = jnp.zeros((SEQ, D), jnp.float32)
    for index in range(N_TP):
        part_grad = grad_proj[:, :, index * group:(index + 1) * group].reshape(SEQ, 3 * group)
        part_weight = proj_weight[:, :, index * group:(index + 1) * group].reshape(D, 3 * group)
        partial_sum = lax.dot_general(part_grad, part_weight, (((1,), (1,)), ((), ())), preferred_element_type=jnp.float32)
        total = total + partial_sum.astype(jnp.bfloat16).astype(jnp.float32)
    return gated, total.astype(jnp.bfloat16)
```

```python
import jax
import jax.numpy as jnp
from jax import lax
from jax.sharding import Mesh
from jax.sharding import PartitionSpec as P

CTX = ("yh", "x", "c")
TP = ("yl", "z")


def from_behind(value, axis, steps):
    count = lax.axis_size(axis)
    first, last = (max(0, -steps), min(count, count - steps))
    return lax.ppermute(value, axis, [(source, source + steps) for source in range(first, last)])


def causal_taps(series, kernel):
    taps = kernel.shape[0]
    length = series.shape[0] - (taps - 1)
    summed = kernel[0] * series[taps - 1 : taps - 1 + length]
    for offset in range(1, taps):
        summed = summed + kernel[offset] * series[taps - 1 - offset : taps - 1 - offset + length]
    return summed


def anti_taps(series, kernel):
    taps = kernel.shape[0]
    length = series.shape[0] - (taps - 1)
    summed = kernel[0] * series[0:length]
    for offset in range(1, taps):
        summed = summed + kernel[offset] * series[offset : offset + length]
    return summed


def featurize(window, feat_taps, inner_taps):
    query_feat = causal_taps(window[6:, 0], feat_taps[0])
    key_feat = causal_taps(window[:, 1], feat_taps[1])
    value_feat = causal_taps(window[:, 2], feat_taps[2])
    inner_conv = causal_taps(key_feat * value_feat, inner_taps)
    return (query_feat, key_feat, value_feat, inner_conv)


def adjoint_rows(series, feat_taps):
    stacked = jnp.stack(
        [
            anti_taps(series[:, 0], feat_taps[0]),
            anti_taps(series[:, 1], feat_taps[1]),
            anti_taps(series[:, 2], feat_taps[2]),
        ],
        axis=1,
    ).astype(jnp.bfloat16)
    return stacked.reshape(stacked.shape[0], 3 * stacked.shape[2])


def local(tokens, proj_weight, feat_taps, inner_taps, grad_out):
    channels = proj_weight.shape[2]
    width = proj_weight.shape[0]
    flat_weight = proj_weight.reshape(width, 3 * channels)
    shard = tokens.shape[0]
    depth = lax.axis_size("z")
    upper = lax.axis_index("yl")
    other = lax.ppermute(tokens, "yl", [(0, 1), (1, 0)])
    pair = jnp.where(
        upper == 0,
        jnp.concatenate([tokens, other], axis=0),
        jnp.concatenate([other, tokens], axis=0),
    )
    projected = jnp.dot(
        lax.all_gather(pair, "z", axis=0, tiled=True),
        flat_weight,
        preferred_element_type=jnp.float32,
    ).astype(jnp.bfloat16)
    row_count = projected.shape[0]
    projected = (
        projected.reshape(depth, 2, shard, 3 * channels)
        .transpose(1, 0, 2, 3)
        .reshape(row_count, 3, channels)
    )
    earlier = from_behind(projected[row_count - 8 :], CTX, 1)
    window = jnp.concatenate([earlier, projected], axis=0).astype(jnp.float32)
    query_feat, key_feat, value_feat, inner_conv = featurize(window, feat_taps, inner_taps)
    gated = (query_feat * inner_conv).astype(jnp.bfloat16)
    grad_f = grad_out.astype(jnp.float32)
    grad_query = grad_f * inner_conv
    grad_inner = grad_f * query_feat
    leading_mix = anti_taps(grad_inner[:8], inner_taps)
    leading = jnp.stack(
        [grad_query[:2], leading_mix * value_feat[6:8], leading_mix * key_feat[6:8]], axis=1
    )
    received, received_inner = from_behind((leading, grad_inner[:6]), CTX, -1)
    grad_mix = anti_taps(jnp.concatenate([grad_inner, received_inner], axis=0), inner_taps)
    grad_key = jnp.concatenate([grad_mix * value_feat[6:], received[:, 1]], axis=0)
    grad_value = jnp.concatenate([grad_mix * key_feat[6:], received[:, 2]], axis=0)
    grad_query = jnp.concatenate([grad_query, received[:, 0]], axis=0)
    grad_series = jnp.stack([grad_query, grad_key, grad_value], axis=1)
    grad_proj = adjoint_rows(grad_series, feat_taps)
    grad_proj = (
        grad_proj.reshape(2, depth, shard, 3 * channels)
        .transpose(1, 0, 2, 3)
        .reshape(row_count, 3 * channels)
    )
    summed = lax.psum_scatter(
        lax.dot_general(
            grad_proj, flat_weight, (((1,), (1,)), ((), ())), preferred_element_type=jnp.float32
        ).astype(jnp.bfloat16),
        "z",
        scatter_dimension=0,
        tiled=True,
    )
    low, high = summed[:shard], summed[shard:]
    mine = jnp.where(upper == 0, low, high)
    theirs = lax.ppermute(jnp.where(upper == 0, high, low), "yl", [(0, 1), (1, 0)])
    grad_tokens = (mine.astype(jnp.float32) + theirs.astype(jnp.float32)).astype(jnp.bfloat16)
    return (gated, grad_tokens)


def solution(mesh):
    grid = Mesh(mesh.devices.reshape(4, 4, 2, 2, 12), CTX + TP)
    in_specs = (
        P(CTX + TP, None),
        P(None, None, TP),
        P(None, None, TP),
        P(None, TP),
        P(CTX, TP),
    )
    out_specs = (P(CTX, TP), P(CTX + TP, None))
    return jax.shard_map(local, mesh=grid, in_specs=in_specs, out_specs=out_specs, check_vma=False)
```

```python
import jax
import jax.numpy as jnp
from jax import lax
from jax.experimental import pallas as pl
from jax.experimental.pallas import tpu as pltpu
from jax.sharding import Mesh
from jax.sharding import PartitionSpec as P

CTX = ("yh", "x", "c")
TP = ("yl", "z")
HALO = 8


def exchange(value, axes, sizes, route):
    total = 1
    for size in sizes:
        total *= size
    pairs = []
    for source in range(total):
        coords, rest = [], source
        for size in reversed(sizes):
            coords.append(rest % size)
            rest //= size
        target = route(*reversed(coords))
        if target is None:
            continue
        flat = 0
        for place, size in zip(target, sizes):
            flat = flat * size + place
        pairs.append((source, flat))
    return lax.ppermute(value, axes, pairs)


def swap_homes(value):
    return exchange(value, ("c", "yl"), (2, 2), lambda c, yl: (yl, c))


def project_kernel(x_ref, w_ref, o_ref):
    o_ref[0] = jnp.dot(x_ref[...], w_ref[0], preferred_element_type=jnp.float32).astype(o_ref.dtype)


def project(rows, weight):
    count, depth = rows.shape
    parts, _, channels = weight.shape
    return pl.pallas_call(
        project_kernel,
        grid=(parts,),
        in_specs=[
            pl.BlockSpec((count, depth), lambda j: (0, 0)),
            pl.BlockSpec((1, depth, channels), lambda j: (j, 0, 0)),
        ],
        out_specs=pl.BlockSpec((1, count, channels), lambda j: (j, 0, 0)),
        out_shape=jax.ShapeDtypeStruct((parts, count, channels), jnp.bfloat16),
        compiler_params=pltpu.CompilerParams(vmem_limit_bytes=40 * 1024 * 1024),
        name="project",
    )(rows, weight)


def spread_kernel(g_ref, w_ref, o_ref):
    contract = (((1,), (1,)), ((), ()))
    total = lax.dot_general(g_ref[0], w_ref[0], contract, preferred_element_type=jnp.float32)
    for part in range(1, g_ref.shape[0]):
        total = total + lax.dot_general(
            g_ref[part], w_ref[part], contract, preferred_element_type=jnp.float32
        )
    o_ref[...] = total.astype(o_ref.dtype)


def spread(grads, weight):
    parts, count, channels = grads.shape
    depth = weight.shape[1]
    block = min(depth, 1024)
    return pl.pallas_call(
        spread_kernel,
        grid=(depth // block,),
        in_specs=[
            pl.BlockSpec((parts, count, channels), lambda i: (0, 0, 0)),
            pl.BlockSpec((parts, block, channels), lambda i: (0, i, 0)),
        ],
        out_specs=pl.BlockSpec((count, block), lambda i: (0, i)),
        out_shape=jax.ShapeDtypeStruct((count, depth), jnp.bfloat16),
        compiler_params=pltpu.CompilerParams(vmem_limit_bytes=40 * 1024 * 1024),
        name="spread",
    )(grads, weight)


def causal(series, taps):
    total = taps[0:1] * series
    for offset in range(1, taps.shape[0]):
        total = total + taps[offset : offset + 1] * pltpu.roll(series, offset, 0)
    return total


def adjoint(series, taps):
    total = taps[0:1] * series
    for offset in range(1, taps.shape[0]):
        total = total + taps[offset : offset + 1] * pltpu.roll(series, series.shape[0] - offset, 0)
    return total


def mix_kernel(proj_ref, prev_ref, next_ref, feat_ref, inner_ref, grad_ref, grad_next_ref, gated_ref, dproj_ref):
    count = proj_ref.shape[1]
    last = HALO + count

    def window(part):
        return jnp.concatenate([prev_ref[part], proj_ref[part], next_ref[part]], axis=0).astype(jnp.float32)

    inner_taps = inner_ref[...]
    query = causal(window(0), feat_ref[0])
    key = causal(window(1), feat_ref[1])
    value = causal(window(2), feat_ref[2])
    inner = causal(key * value, inner_taps)
    gated_ref[...] = (query * inner)[HALO:last].astype(gated_ref.dtype)
    grad_next = grad_next_ref[...]
    grad = jnp.concatenate([jnp.zeros_like(grad_next), grad_ref[...], grad_next], axis=0).astype(jnp.float32)
    mixed = adjoint(grad * query, inner_taps)
    dproj_ref[0] = adjoint(grad * inner, feat_ref[0])[HALO:last].astype(dproj_ref.dtype)
    dproj_ref[1] = adjoint(mixed * value, feat_ref[1])[HALO:last].astype(dproj_ref.dtype)
    dproj_ref[2] = adjoint(mixed * key, feat_ref[2])[HALO:last].astype(dproj_ref.dtype)


def mix(proj, prev, following, feat, inner, grad, grad_next):
    parts, count, channels = proj.shape
    lanes = min(channels, 128)

    def whole(shape):
        lead = len(shape) - 1
        return pl.BlockSpec(shape[:-1] + (lanes,), lambda i: (0,) * lead + (i,))

    operands = (proj, prev, following, feat, inner, grad, grad_next)
    return pl.pallas_call(
        mix_kernel,
        grid=(channels // lanes,),
        in_specs=[whole(operand.shape) for operand in operands],
        out_specs=[whole((count, channels)), whole(proj.shape)],
        out_shape=[
            jax.ShapeDtypeStruct((count, channels), jnp.bfloat16),
            jax.ShapeDtypeStruct(proj.shape, jnp.bfloat16),
        ],
        compiler_params=pltpu.CompilerParams(vmem_limit_bytes=40 * 1024 * 1024),
        name="mix",
    )(*operands)


def build(sizes):
    ring = sizes[0] * 2

    strips = sizes[0] * sizes[1] * 4

    def along(value, step):
        def route(yh, x, c, yl):
            strip = ((yh * sizes[1] + x) * 2 + yl) * 2 + c + step
            if not 0 <= strip < strips:
                return None
            return (strip // 4 // sizes[1], strip // 4 % sizes[1], strip % 2, strip // 2 % 2)

        return exchange(value, ("yh", "x", "c", "yl"), (sizes[0], sizes[1], 2, 2), route)

    def local(tokens, proj_weight, feat_taps, inner_taps, grad_out):
        upper = lax.axis_index("yl")
        core = lax.axis_index("c")
        depth = proj_weight.shape[0]

        gathered = lax.all_gather(swap_homes(tokens), "z", axis=0, tiled=True)

        planes = proj_weight.transpose(1, 0, 2)
        half = depth // 2
        sent = lax.dynamic_slice_in_dim(planes, core * half, half, 1)

        def beside(yh, c, yl):
            place = (yh * 2 + yl + (1 if c else ring - 1)) % ring
            return (place // 2, c, place % 2)

        came = exchange(sent, ("yh", "c", "yl"), (sizes[0], 2, 2), beside)
        rest = lax.ppermute(came, "c", [(0, 1), (1, 0)])
        other_planes = jnp.where(
            core == 0,
            jnp.concatenate([came, rest], axis=1),
            jnp.concatenate([rest, came], axis=1),
        )

        def both(mine, theirs, axis):
            return jnp.where(
                upper == 0,
                jnp.concatenate([mine, theirs], axis=axis),
                jnp.concatenate([theirs, mine], axis=axis),
            )

        def other(value):
            return lax.ppermute(value, "yl", [(0, 1), (1, 0)])

        weight = both(planes, other_planes, 2)
        feat = both(feat_taps, other(feat_taps), 2)
        inner = both(inner_taps, other(inner_taps), 1)

        count = grad_out.shape[0] // 2
        near = lax.dynamic_slice_in_dim(grad_out, upper * count, count, 0)
        far = lax.dynamic_slice_in_dim(grad_out, (1 - upper) * count, count, 0)
        near = swap_homes(near)
        far = exchange(far, ("c", "yl"), (2, 2), lambda c, yl: (1 - yl, c))
        grad = jnp.where(
            core == 0,
            jnp.concatenate([near, far], axis=1),
            jnp.concatenate([far, near], axis=1),
        )
        grad_next = along(grad[:HALO], -1)

        proj = project(gathered, weight)
        prev = along(proj[:, count - HALO :], 1)
        following = along(proj[:, :HALO], -1)
        gated, dproj = mix(proj, prev, following, feat, inner, grad, grad_next)

        grad_tokens = lax.psum_scatter(spread(dproj, weight), "z", scatter_dimension=0, tiled=True)

        channels = inner_taps.shape[1]
        first, second = gated[:, :channels], gated[:, channels:]
        near = swap_homes(jnp.where(core == 0, first, second))
        far = exchange(
            jnp.where(core == 0, second, first), ("c", "yl"), (2, 2), lambda c, yl: (yl, 1 - c)
        )
        gated = jnp.where(
            upper == 0,
            jnp.concatenate([near, far], axis=0),
            jnp.concatenate([far, near], axis=0),
        )
        return (gated, swap_homes(grad_tokens))

    return local


def solution(mesh):
    sizes = (4, 4, 2, 2, 12)
    grid = Mesh(mesh.devices.reshape(sizes), CTX + TP)
    in_specs = (
        P(CTX + TP, None),
        P(None, None, TP),
        P(None, None, TP),
        P(None, TP),
        P(CTX, TP),
    )
    out_specs = (P(CTX, TP), P(CTX + TP, None))
    return jax.shard_map(build(sizes), mesh=grid, in_specs=in_specs, out_specs=out_specs, check_vma=False)
```

```python
import jax
import jax.numpy as jnp
from jax import lax
from jax.experimental import pallas as pl
from jax.experimental.pallas import tpu as pltpu
from jax.sharding import Mesh
from jax.sharding import PartitionSpec as P

CTX = ("yh", "x", "c")
TP = ("yl", "zh", "zl")
RING = ("zh", "zl")
HALO = 8
SHARD = 24


def exchange(value, axes, sizes, route):
    total = 1
    for size in sizes:
        total *= size
    pairs = []
    for source in range(total):
        coords, rest = [], source
        for size in reversed(sizes):
            coords.append(rest % size)
            rest //= size
        target = route(*reversed(coords))
        if target is None:
            continue
        flat = 0
        for place, size in zip(target, sizes):
            flat = flat * size + place
        pairs.append((source, flat))
    return lax.ppermute(value, axes, pairs)


def swap_homes(value):
    return exchange(value, ("c", "yl"), (2, 2), lambda c, yl: (yl, c))


def fetch(source, target, sems):
    copies = [
        pltpu.make_async_copy(source(i), target(i), sems.at[i]) for i in range(sems.shape[0])
    ]
    for copy in copies:
        copy.start()
    return copies


def project_own_kernel(x_ref, w_ref, o_ref, w_buf, sems):
    copies = fetch(lambda j: w_ref.at[j], lambda j: w_buf.at[j], sems)
    for part, copy in enumerate(copies):
        copy.wait()
        total = jnp.dot(x_ref[...], w_buf[part], preferred_element_type=jnp.float32)
        o_ref[part] = total.astype(o_ref.dtype)


def project_rest_kernel(lane_ref, plus_ref, minus_ref, own_ref, w_ref, o_ref, head_ref, tail_ref, w_buf, sems):
    copies = fetch(lambda j: w_ref.at[j], lambda j: w_buf.at[j], sems)
    rows = jnp.concatenate([plus_ref[...], minus_ref[...]], axis=0)
    count = plus_ref.shape[0]
    lane = lane_ref[0]
    for part, copy in enumerate(copies):
        copy.wait()
        total = jnp.dot(rows, w_buf[part], preferred_element_type=jnp.float32)
        own = own_ref[part].astype(jnp.float32)
        plus, minus = total[:count], total[count:]
        o_ref[part] = total.astype(o_ref.dtype)

        def pick(chosen, start):
            third = [block[start : start + HALO] for block in (own, plus, minus)]
            ahead = lax.rem(lane + 1, 3)
            value = jnp.where(ahead == chosen, third[1], third[2])
            return jnp.where(lane == chosen, third[0], value)

        head_ref[part] = pick(0, 0).astype(head_ref.dtype)
        tail_ref[part] = pick(2, count - HALO).astype(tail_ref.dtype)


def vmem():
    return pl.BlockSpec(memory_space=pltpu.MemorySpace.VMEM)


def smem():
    return pl.BlockSpec(memory_space=pltpu.MemorySpace.SMEM)


def hbm():
    return pl.BlockSpec(memory_space=pltpu.MemorySpace.HBM)


PARAMS = pltpu.CompilerParams(vmem_limit_bytes=48 * 1024 * 1024)


def project_own(rows, weight):
    parts, _, channels = weight.shape
    return pl.pallas_call(
        project_own_kernel,
        in_specs=[vmem(), hbm()],
        out_specs=vmem(),
        out_shape=jax.ShapeDtypeStruct((parts, rows.shape[0], channels), jnp.bfloat16),
        scratch_shapes=[pltpu.VMEM(weight.shape, weight.dtype), pltpu.SemaphoreType.DMA((parts,))],
        compiler_params=PARAMS,
        name="project_own",
    )(rows, weight)


def project_rest(lane, plus, minus, own, weight):
    parts, _, channels = weight.shape
    edge = jax.ShapeDtypeStruct((parts, HALO, channels), jnp.bfloat16)
    return pl.pallas_call(
        project_rest_kernel,
        in_specs=[smem(), vmem(), vmem(), vmem(), hbm()],
        out_specs=[vmem(), vmem(), vmem()],
        out_shape=[
            jax.ShapeDtypeStruct((parts, 2 * plus.shape[0], channels), jnp.bfloat16),
            edge,
            edge,
        ],
        scratch_shapes=[pltpu.VMEM(weight.shape, weight.dtype), pltpu.SemaphoreType.DMA((parts,))],
        compiler_params=PARAMS,
        name="project_rest",
    )(lane, plus, minus, own, weight)


def join_kernel(place_ref, mine_ref, came_ref, rest_ref, o_ref):
    lanes = mine_ref.shape[2]
    half = pl.program_id(1)
    theirs = jnp.where(half == place_ref[1], came_ref[0], rest_ref[0])
    mine = mine_ref[0]
    first = place_ref[0] == 0
    o_ref[0, :, :lanes] = jnp.where(first, mine, theirs)
    o_ref[0, :, lanes:] = jnp.where(first, theirs, mine)


def join(place, mine, came, rest):
    parts, depth, lanes = mine.shape
    half = depth // 2
    return pl.pallas_call(
        join_kernel,
        grid=(parts, 2),
        in_specs=[
            smem(),
            pl.BlockSpec((1, half, lanes), lambda j, k: (j, k, 0)),
            pl.BlockSpec((1, half, lanes), lambda j, k: (j, 0, 0)),
            pl.BlockSpec((1, half, lanes), lambda j, k: (j, 0, 0)),
        ],
        out_specs=pl.BlockSpec((1, half, 2 * lanes), lambda j, k: (j, k, 0)),
        out_shape=jax.ShapeDtypeStruct((parts, depth, 2 * lanes), mine.dtype),
        compiler_params=PARAMS,
        name="join",
    )(place, mine, came, rest)


def causal(series, taps):
    total = taps[0:1] * series
    for offset in range(1, taps.shape[0]):
        total = total + taps[offset : offset + 1] * pltpu.roll(series, offset, 0)
    return total


def adjoint(series, taps):
    total = taps[0:1] * series
    for offset in range(1, taps.shape[0]):
        total = total + taps[offset : offset + 1] * pltpu.roll(series, series.shape[0] - offset, 0)
    return total


def mix_kernel(
    lane_ref, own_ref, rest_ref, prev_ref, next_ref, feat_ref, inner_ref, grad_ref, grad_next_ref, w_ref,
    gated_ref, keep_ref, plus_ref, minus_ref,
    window, back, w_buf, sems,
):
    parts, count, channels = own_ref.shape
    total_rows = grad_ref.shape[0]
    last = HALO + total_rows
    block = w_buf.shape[1] // sems.shape[0]
    copies = fetch(
        lambda i: w_ref.at[:, pl.ds(i * block, block), :],
        lambda i: w_buf.at[:, pl.ds(i * block, block), :],
        sems,
    )
    lane = lane_ref[0]
    groups = [lane, lax.rem(lane + 1, 3), lax.rem(lane + 2, 3)]
    shard = SHARD
    members = count // shard

    def start(group, member):
        return pl.multiple_of((3 * member + groups[group]) * shard, 8)

    for part in range(parts):
        window[part, :HALO] = prev_ref[part].astype(jnp.float32)
        window[part, last:] = next_ref[part].astype(jnp.float32)
        blocks = (own_ref[part], rest_ref[part, :count], rest_ref[part, count:])
        for group, rows in enumerate(blocks):
            rows = rows.astype(jnp.float32)
            for member in range(members):
                window[part, pl.ds(start(group, member) + HALO, shard)] = rows[
                    member * shard : (member + 1) * shard
                ]
    lanes = min(channels, 128)
    for side in range(channels // lanes):
        cut = slice(side * lanes, (side + 1) * lanes)
        inner_taps = inner_ref[:, cut]
        feat = [feat_ref[part][:, cut] for part in range(parts)]
        query = causal(window[0, :, cut], feat[0])
        key = causal(window[1, :, cut], feat[1])
        value = causal(window[2, :, cut], feat[2])
        inner = causal(key * value, inner_taps)
        gated_ref[:, cut] = (query * inner)[HALO:last].astype(gated_ref.dtype)
        grad_next = grad_next_ref[:, cut]
        grad = jnp.concatenate([jnp.zeros_like(grad_next), grad_ref[:, cut], grad_next], axis=0)
        grad = grad.astype(jnp.float32)
        mixed = adjoint(grad * query, inner_taps)
        back[0, :, cut] = adjoint(grad * inner, feat[0])[HALO:last]
        back[1, :, cut] = adjoint(mixed * value, feat[1])[HALO:last]
        back[2, :, cut] = adjoint(mixed * key, feat[2])[HALO:last]
    left = [
        jnp.concatenate(
            [
                back[part, pl.ds(start(group, member), shard)]
                for group in range(3)
                for member in range(members)
            ],
            axis=0,
        ).astype(jnp.bfloat16)
        for part in range(parts)
    ]
    contract = (((1,), (1,)), ((), ()))
    for i, copy in enumerate(copies):
        copy.wait()
        cut = slice(i * block, (i + 1) * block)
        total = lax.dot_general(left[0], w_buf[0, cut], contract, preferred_element_type=jnp.float32)
        for part in range(1, parts):
            total = total + lax.dot_general(
                left[part], w_buf[part, cut], contract, preferred_element_type=jnp.float32
            )
        keep_ref[:, cut] = total[:count]
        plus_ref[:, cut] = total[count : 2 * count].astype(plus_ref.dtype)
        minus_ref[:, cut] = total[2 * count :].astype(minus_ref.dtype)


def mix(lane, own, rest, prev, following, feat, inner, grad, grad_next, weight):
    parts, count, channels = own.shape
    depth = weight.shape[1]
    rows = grad.shape[0]
    steps = max(1, depth // 512)
    return pl.pallas_call(
        mix_kernel,
        in_specs=[smem()] + [vmem()] * 8 + [hbm()],
        out_specs=[vmem()] * 4,
        out_shape=[
            jax.ShapeDtypeStruct((rows, channels), jnp.bfloat16),
            jax.ShapeDtypeStruct((count, depth), jnp.float32),
            jax.ShapeDtypeStruct((count, depth), jnp.bfloat16),
            jax.ShapeDtypeStruct((count, depth), jnp.bfloat16),
        ],
        scratch_shapes=[
            pltpu.VMEM((parts, rows + 2 * HALO, channels), jnp.float32),
            pltpu.VMEM((parts, rows, channels), jnp.float32),
            pltpu.VMEM(weight.shape, weight.dtype),
            pltpu.SemaphoreType.DMA((steps,)),
        ],
        compiler_params=PARAMS,
        name="mix",
    )(lane, own, rest, prev, following, feat, inner, grad, grad_next, weight)


def build(sizes):
    ring = sizes[0] * 2

    strips = sizes[0] * sizes[1] * 4

    def along(value, step):
        def route(yh, x, c, yl):
            strip = ((yh * sizes[1] + x) * 2 + yl) * 2 + c + step
            if not 0 <= strip < strips:
                return None
            return (strip // 4 // sizes[1], strip // 4 % sizes[1], strip % 2, strip // 2 % 2)

        return exchange(value, ("yh", "x", "c", "yl"), (sizes[0], sizes[1], 2, 2), route)

    spots = sizes[4] * sizes[5]

    def turn(value, step):
        return lax.ppermute(value, RING, [(z, (z + step) % spots) for z in range(spots)])

    def local(tokens, proj_weight, feat_taps, inner_taps, grad_out):
        upper = lax.axis_index("yl")
        core = lax.axis_index("c")
        lane = lax.axis_index("zl").astype(jnp.int32).reshape(1)
        width = proj_weight.shape[0]
        channels = inner_taps.shape[1]

        rehomed = swap_homes(tokens)
        padded = jnp.concatenate([rehomed, rehomed[:8]], axis=0)
        own = lax.all_gather(padded, "zh", axis=0, tiled=False)
        own = own[:, :SHARD].reshape(sizes[4] * SHARD, width)

        planes = proj_weight.transpose(1, 0, 2)
        half = width // 2
        sent = lax.dynamic_slice_in_dim(planes, core * half, half, 1)

        def beside(yh, c, yl):
            place = (yh * 2 + yl + (1 if c else ring - 1)) % ring
            return (place // 2, c, place % 2)

        came = exchange(sent, ("yh", "c", "yl"), (sizes[0], 2, 2), beside)

        def both(mine, theirs, axis):
            return jnp.where(
                upper == 0,
                jnp.concatenate([mine, theirs], axis=axis),
                jnp.concatenate([theirs, mine], axis=axis),
            )

        taps = jnp.concatenate([feat_taps.reshape(9, channels), inner_taps], axis=0)
        taps = both(taps, lax.ppermute(taps, "yl", [(0, 1), (1, 0)]), 1)
        feat = taps[:9].reshape(3, 3, 2 * channels)
        inner = taps[9:]

        count = grad_out.shape[0] // 2
        near = lax.dynamic_slice_in_dim(grad_out, upper * count, count, 0)
        far = lax.dynamic_slice_in_dim(grad_out, (1 - upper) * count, count, 0)
        near = swap_homes(near)
        far = exchange(far, ("c", "yl"), (2, 2), lambda c, yl: (1 - yl, c))
        grad = jnp.where(
            core == 0,
            jnp.concatenate([near, far], axis=1),
            jnp.concatenate([far, near], axis=1),
        )
        grad_next = along(grad[:HALO], -1)

        came, grad, grad_next, feat, inner = lax.optimization_barrier((came, grad, grad_next, feat, inner))
        rest = lax.ppermute(came, "c", [(0, 1), (1, 0)])
        weight = join(jnp.stack([upper, core]).astype(jnp.int32), planes, came, rest)

        plus, minus = turn(own, -1), turn(own, 1)
        proj_own = project_own(own, weight)
        proj_rest, head, tail = project_rest(lane, plus, minus, proj_own, weight)
        prev = along(tail, 1)
        following = along(head, -1)
        gated, keep, to_plus, to_minus = mix(
            lane, proj_own, proj_rest, prev, following, feat, inner, grad, grad_next, weight
        )
        summed = keep + turn(to_plus, 1).astype(jnp.float32) + turn(to_minus, -1).astype(jnp.float32)
        grad_tokens = lax.psum_scatter(
            summed.astype(jnp.bfloat16), "zh", scatter_dimension=0, tiled=True
        )

        first, second = gated[:, :channels], gated[:, channels:]
        near = swap_homes(jnp.where(core == 0, first, second))
        far = exchange(
            jnp.where(core == 0, second, first), ("c", "yl"), (2, 2), lambda c, yl: (yl, 1 - c)
        )
        gated = jnp.where(
            upper == 0,
            jnp.concatenate([near, far], axis=0),
            jnp.concatenate([far, near], axis=0),
        )
        grad_tokens, gated = lax.optimization_barrier((grad_tokens, gated))
        return (gated, swap_homes(grad_tokens))

    return local


def solution(mesh):
    sizes = (4, 4, 2, 2, 4, 3)
    grid = Mesh(mesh.devices.reshape(sizes), CTX + TP)
    in_specs = (
        P(CTX + TP, None),
        P(None, None, TP),
        P(None, None, TP),
        P(None, TP),
        P(CTX, TP),
    )
    out_specs = (P(CTX, TP), P(CTX + TP, None))
    return jax.shard_map(build(sizes), mesh=grid, in_specs=in_specs, out_specs=out_specs, check_vma=False)
```

```python
import jax
import jax.numpy as jnp
from jax import lax
from jax.experimental import pallas as pl
from jax.experimental.pallas import tpu as pltpu
from jax.sharding import Mesh
from jax.sharding import PartitionSpec as P

CTX = ("yh", "x", "c")
TP = ("yl", "z")
HALO = 8
TOP = 13.0


def exchange(value, axes, sizes, route):
    total = 1
    for size in sizes:
        total *= size
    pairs = []
    for source in range(total):
        coords, rest = [], source
        for size in reversed(sizes):
            coords.append(rest % size)
            rest //= size
        target = route(*reversed(coords))
        if target is None:
            continue
        flat = 0
        for place, size in zip(target, sizes):
            flat = flat * size + place
        pairs.append((source, flat))
    return lax.ppermute(value, axes, pairs)


def swap_homes(value):
    return exchange(value, ("c", "yl"), (2, 2), lambda c, yl: (yl, c))


def vmem():
    return pl.BlockSpec(memory_space=pltpu.MemorySpace.VMEM)


def smem():
    return pl.BlockSpec(memory_space=pltpu.MemorySpace.SMEM)


def hbm():
    return pl.BlockSpec(memory_space=pltpu.MemorySpace.HBM)


PARAMS = pltpu.CompilerParams(vmem_limit_bytes=48 * 1024 * 1024)


def slots(upper_ref, lanes):
    upper = upper_ref[0]
    return pl.multiple_of(upper * lanes, lanes), pl.multiple_of((1 - upper) * lanes, lanes)


def project_kernel(upper_ref, x_ref, grad_ref, mine_ref, low_ref, high_ref, o_ref, head_ref, tail_ref, w_buf, sems):
    parts, depth, lanes = mine_ref.shape
    half = depth // 2
    own, other = slots(upper_ref, lanes)
    copies = []
    for j in range(parts):
        moves = (
            (mine_ref.at[j], w_buf.at[j, :, pl.ds(own, lanes)]),
            (low_ref.at[j], w_buf.at[j, pl.ds(0, half), pl.ds(other, lanes)]),
            (high_ref.at[j], w_buf.at[j, pl.ds(half, half), pl.ds(other, lanes)]),
        )
        copies.append(
            [pltpu.make_async_copy(src, dst, sems.at[j, k]) for k, (src, dst) in enumerate(moves)]
        )
        for copy in copies[-1]:
            copy.start()
    rows = x_ref[:, :depth]
    scale = jnp.exp2(x_ref[:, depth : depth + 1].astype(jnp.float32) - TOP)
    count = rows.shape[0]
    for j in range(parts):
        for copy in copies[j]:
            copy.wait()
        total = jnp.dot(rows, w_buf[j], preferred_element_type=jnp.float32) * scale
        o_ref[j] = total.astype(o_ref.dtype)
        head_ref[j] = total[:HALO].astype(head_ref.dtype)
        tail_ref[j] = total[count - HALO :].astype(tail_ref.dtype)
    head_ref[parts] = grad_ref[:HALO]


def project(upper, rows, grad, mine, low, high):
    parts, depth, lanes = mine.shape
    count = rows.shape[0]
    return pl.pallas_call(
        project_kernel,
        in_specs=[smem(), vmem(), vmem(), hbm(), hbm(), hbm()],
        out_specs=[vmem()] * 3,
        out_shape=[
            jax.ShapeDtypeStruct((parts, count, 2 * lanes), jnp.bfloat16),
            jax.ShapeDtypeStruct((parts + 1, HALO, 2 * lanes), jnp.bfloat16),
            jax.ShapeDtypeStruct((parts, HALO, 2 * lanes), jnp.bfloat16),
        ],
        scratch_shapes=[
            pltpu.VMEM((parts, depth, 2 * lanes), mine.dtype),
            pltpu.SemaphoreType.DMA((parts, 3)),
        ],
        compiler_params=PARAMS,
        name="project",
    )(upper, rows, grad, mine, low, high)


def causal(series, taps):
    total = taps[0:1] * series
    for offset in range(1, taps.shape[0]):
        total = total + taps[offset : offset + 1] * pltpu.roll(series, offset, 0)
    return total


def adjoint(series, taps):
    total = taps[0:1] * series
    for offset in range(1, taps.shape[0]):
        total = total + taps[offset : offset + 1] * pltpu.roll(series, series.shape[0] - offset, 0)
    return total


def mix_kernel(
    upper_ref, proj_ref, prev_ref, next_ref, feat_ref, inner_ref, grad_ref, mine_ref, low_ref, high_ref,
    gated_ref, o_ref, w_buf, back, sems,
):
    parts, depth, lanes = mine_ref.shape
    count = grad_ref.shape[0]
    last = HALO + count
    steps = sems.shape[0]
    block = depth // steps
    own, other = slots(upper_ref, lanes)
    copies = []
    for i in range(steps):
        begin = i * block
        source, shift = (low_ref, begin) if begin < depth // 2 else (high_ref, begin - depth // 2)
        copies.append(
            (
                pltpu.make_async_copy(
                    mine_ref.at[:, pl.ds(begin, block), :],
                    w_buf.at[:, pl.ds(begin, block), pl.ds(own, lanes)],
                    sems.at[i, 0],
                ),
                pltpu.make_async_copy(
                    source.at[:, pl.ds(shift, block), :],
                    w_buf.at[:, pl.ds(begin, block), pl.ds(other, lanes)],
                    sems.at[i, 1],
                ),
            )
        )
        for copy in copies[-1]:
            copy.start()
    for side in range(2):
        cut = slice(side * lanes, (side + 1) * lanes)

        def window(part):
            rows = [prev_ref[part, :, cut], proj_ref[part, :, cut], next_ref[part, :, cut]]
            return jnp.concatenate(rows, axis=0).astype(jnp.float32)

        inner_taps = inner_ref[:, cut]
        feat = [feat_ref[part][:, cut] for part in range(parts)]
        query = causal(window(0), feat[0])
        key = causal(window(1), feat[1])
        value = causal(window(2), feat[2])
        inner = causal(key * value, inner_taps)
        gated_ref[:, cut] = (query * inner)[HALO:last].astype(gated_ref.dtype)
        grad_next = next_ref[parts, :, cut]
        grad = jnp.concatenate([jnp.zeros_like(grad_next), grad_ref[:, cut], grad_next], axis=0)
        grad = grad.astype(jnp.float32)
        mixed = adjoint(grad * query, inner_taps)
        back[0, :, cut] = adjoint(grad * inner, feat[0])[HALO:last].astype(back.dtype)
        back[1, :, cut] = adjoint(mixed * value, feat[1])[HALO:last].astype(back.dtype)
        back[2, :, cut] = adjoint(mixed * key, feat[2])[HALO:last].astype(back.dtype)
    contract = (((1,), (1,)), ((), ()))
    for i in range(steps):
        for copy in copies[i]:
            copy.wait()
        cut = slice(i * block, (i + 1) * block)
        total = lax.dot_general(back[0], w_buf[0, cut], contract, preferred_element_type=jnp.float32)
        for part in range(1, parts):
            total = total + lax.dot_general(
                back[part], w_buf[part, cut], contract, preferred_element_type=jnp.float32
            )
        o_ref[:, cut] = total.astype(o_ref.dtype)


def mix(upper, proj, prev, following, feat, inner, grad, mine, low, high):
    parts, depth, lanes = mine.shape
    count = grad.shape[0]
    steps = 8
    return pl.pallas_call(
        mix_kernel,
        in_specs=[smem()] + [vmem()] * 6 + [hbm()] * 3,
        out_specs=[vmem(), vmem()],
        out_shape=[
            jax.ShapeDtypeStruct((count, 2 * lanes), jnp.bfloat16),
            jax.ShapeDtypeStruct((count, depth), jnp.bfloat16),
        ],
        scratch_shapes=[
            pltpu.VMEM((parts, depth, 2 * lanes), mine.dtype),
            pltpu.VMEM((parts, count, 2 * lanes), jnp.bfloat16),
            pltpu.SemaphoreType.DMA((steps, 2)),
        ],
        compiler_params=PARAMS,
        name="mix",
    )(upper, proj, prev, following, feat, inner, grad, mine, low, high)


def encode(tokens):
    wide = tokens.astype(jnp.float32)
    peak = jnp.max(jnp.abs(wide), axis=1, keepdims=True)
    power = jnp.clip(jnp.floor(jnp.log2(jnp.maximum(peak, 1e-37))), -110.0, 110.0)
    scaled = wide * jnp.exp2(TOP - power)
    return jnp.concatenate(
        [scaled, jnp.broadcast_to(power, (tokens.shape[0], 128))], axis=1
    ).astype(jnp.float16)


def build(sizes):
    ring = sizes[0] * 2

    strips = sizes[0] * sizes[1] * 4

    def along(value, step):
        def route(yh, x, c, yl):
            strip = ((yh * sizes[1] + x) * 2 + yl) * 2 + c + step
            if not 0 <= strip < strips:
                return None
            return (strip // 4 // sizes[1], strip // 4 % sizes[1], strip % 2, strip // 2 % 2)

        return exchange(value, ("yh", "x", "c", "yl"), (sizes[0], sizes[1], 2, 2), route)

    def local(tokens, proj_weight, feat_taps, inner_taps, grad_out):
        upper = lax.axis_index("yl")
        core = lax.axis_index("c")
        width = proj_weight.shape[0]
        channels = inner_taps.shape[1]
        flag = upper.astype(jnp.int32).reshape(1)

        planes = proj_weight.transpose(1, 0, 2)
        half = width // 2
        low, high = planes[:, :half], planes[:, half:]
        count = grad_out.shape[0] // 2
        near = lax.dynamic_slice_in_dim(grad_out, upper * count, count, 0)
        far = lax.dynamic_slice_in_dim(grad_out, (1 - upper) * count, count, 0)
        taps = jnp.concatenate([feat_taps.reshape(9, channels), inner_taps], axis=0)

        rehomed = swap_homes(encode(tokens))
        rehomed, low, high, near, far, sent_taps = lax.optimization_barrier(
            (rehomed, low, high, near, far, taps)
        )

        def beside(step):
            def route(yh, yl):
                place = (yh * 2 + yl + step) % ring
                return (place // 2, place % 2)

            return route

        low = exchange(low, ("yh", "yl"), (sizes[0], 2), beside(-1))
        high = exchange(high, ("yh", "yl"), (sizes[0], 2), beside(1))

        def both(mine, theirs, axis):
            return jnp.where(
                upper == 0,
                jnp.concatenate([mine, theirs], axis=axis),
                jnp.concatenate([theirs, mine], axis=axis),
            )

        near = swap_homes(near)
        far = exchange(far, ("c", "yl"), (2, 2), lambda c, yl: (1 - yl, c))
        came_taps = lax.ppermute(sent_taps, "yl", [(0, 1), (1, 0)])
        rehomed, near, far, came_taps = lax.optimization_barrier((rehomed, near, far, came_taps))
        gathered = lax.all_gather(rehomed, "z", axis=0, tiled=True).astype(jnp.bfloat16)
        taps = both(taps, came_taps, 1)
        feat = taps[:9].reshape(3, 3, 2 * channels)
        inner = taps[9:]
        grad = jnp.where(
            core == 0,
            jnp.concatenate([near, far], axis=1),
            jnp.concatenate([far, near], axis=1),
        )

        proj, head, tail = project(flag, gathered, grad, planes, low, high)
        prev = along(tail, 1)
        following = along(head, -1)
        gated, spread = mix(flag, proj, prev, following, feat, inner, grad, planes, low, high)
        grad_tokens = lax.psum_scatter(spread, "z", scatter_dimension=0, tiled=True)

        first, second = gated[:, :channels], gated[:, channels:]
        near = swap_homes(jnp.where(core == 0, first, second))
        far = exchange(
            jnp.where(core == 0, second, first), ("c", "yl"), (2, 2), lambda c, yl: (yl, 1 - c)
        )
        gated = jnp.where(
            upper == 0,
            jnp.concatenate([near, far], axis=0),
            jnp.concatenate([far, near], axis=0),
        )
        grad_tokens, gated = lax.optimization_barrier((grad_tokens, gated))
        return (gated, swap_homes(grad_tokens))

    return local


def solution(mesh):
    sizes = (4, 4, 2, 2, 12)
    grid = Mesh(mesh.devices.reshape(sizes), CTX + TP)
    in_specs = (
        P(CTX + TP, None),
        P(None, None, TP),
        P(None, None, TP),
        P(None, TP),
        P(CTX, TP),
    )
    out_specs = (P(CTX, TP), P(CTX + TP, None))
    return jax.shard_map(build(sizes), mesh=grid, in_specs=in_specs, out_specs=out_specs, check_vma=False)
```

```python
import jax
import jax.numpy as jnp
from jax import lax
from jax.experimental import pallas as pl
from jax.experimental.pallas import tpu as pltpu
from jax.sharding import Mesh
from jax.sharding import PartitionSpec as P

CTX = ("yh", "x", "c")
TP = ("yl", "z")
HALO = 8
TOP = 13.0


def exchange(value, axes, sizes, route):
    total = 1
    for size in sizes:
        total *= size
    pairs = []
    for source in range(total):
        coords, rest = [], source
        for size in reversed(sizes):
            coords.append(rest % size)
            rest //= size
        target = route(*reversed(coords))
        if target is None:
            continue
        flat = 0
        for place, size in zip(target, sizes):
            flat = flat * size + place
        pairs.append((source, flat))
    return lax.ppermute(value, axes, pairs)


def swap_homes(value):
    return exchange(value, ("c", "yl"), (2, 2), lambda c, yl: (yl, c))


def vmem():
    return pl.BlockSpec(memory_space=pltpu.MemorySpace.VMEM)


def smem():
    return pl.BlockSpec(memory_space=pltpu.MemorySpace.SMEM)


def hbm():
    return pl.BlockSpec(memory_space=pltpu.MemorySpace.HBM)


PARAMS = pltpu.CompilerParams(vmem_limit_bytes=24 * 1024 * 1024)


def slots(upper_ref, lanes):
    upper = upper_ref[0]
    return pl.multiple_of(upper * lanes, lanes), pl.multiple_of((1 - upper) * lanes, lanes)


def project_kernel(upper_ref, x_ref, packed_ref, mine_ref, theirs_ref, o_ref, head_ref, tail_ref, w_buf, sems):
    parts, depth, lanes = mine_ref.shape
    own, other = slots(upper_ref, lanes)
    copies = []
    for j in range(parts):
        moves = (
            (mine_ref.at[j], w_buf.at[j, :, pl.ds(own, lanes)]),
            (theirs_ref.at[j], w_buf.at[j, :, pl.ds(other, lanes)]),
        )
        copies.append(
            [pltpu.make_async_copy(src, dst, sems.at[j, k]) for k, (src, dst) in enumerate(moves)]
        )
        for copy in copies[-1]:
            copy.start()
    rows = x_ref[:, :depth]
    scale = jnp.exp2(x_ref[:, depth : depth + 1].astype(jnp.float32) - TOP)
    count = rows.shape[0]
    for j in range(parts):
        for copy in copies[j]:
            copy.wait()
        total = jnp.dot(rows, w_buf[j], preferred_element_type=jnp.float32) * scale
        o_ref[j] = total.astype(o_ref.dtype)
        head_ref[j] = total[:HALO].astype(head_ref.dtype)
        tail_ref[j] = total[count - HALO :].astype(tail_ref.dtype)
    head_ref[parts] = packed_ref[:HALO].astype(head_ref.dtype)


def project(upper, rows, packed, mine, theirs):
    parts, depth, lanes = mine.shape
    count = rows.shape[0]
    return pl.pallas_call(
        project_kernel,
        in_specs=[smem(), vmem(), vmem(), hbm(), hbm()],
        out_specs=[vmem()] * 3,
        out_shape=[
            jax.ShapeDtypeStruct((parts, count, 2 * lanes), jnp.bfloat16),
            jax.ShapeDtypeStruct((parts + 1, HALO, 2 * lanes), jnp.bfloat16),
            jax.ShapeDtypeStruct((parts, HALO, 2 * lanes), jnp.bfloat16),
        ],
        scratch_shapes=[
            pltpu.VMEM((parts, depth, 2 * lanes), mine.dtype),
            pltpu.SemaphoreType.DMA((parts, 2)),
        ],
        compiler_params=PARAMS,
        name="project",
    )(upper, rows, packed, mine, theirs)


def causal(series, taps):
    total = taps[0:1] * series
    for offset in range(1, taps.shape[0]):
        total = total + taps[offset : offset + 1] * pltpu.roll(series, offset, 0)
    return total


def adjoint(series, taps):
    total = taps[0:1] * series
    for offset in range(1, taps.shape[0]):
        total = total + taps[offset : offset + 1] * pltpu.roll(series, series.shape[0] - offset, 0)
    return total


def mix_kernel(
    upper_ref, proj_ref, prev_ref, next_ref, packed_ref, mine_ref, theirs_ref,
    gated_ref, o_ref, w_buf, back, o_buf, sems,
):
    parts, depth, lanes = mine_ref.shape
    count = proj_ref.shape[1]
    last = HALO + count
    steps = sems.shape[0]
    block = depth // steps
    own, other = slots(upper_ref, lanes)
    copies = []
    for i in range(steps):
        begin = i * block
        copies.append(
            (
                pltpu.make_async_copy(
                    mine_ref.at[:, pl.ds(begin, block), :],
                    w_buf.at[:, pl.ds(begin, block), pl.ds(own, lanes)],
                    sems.at[i, 0],
                ),
                pltpu.make_async_copy(
                    theirs_ref.at[:, pl.ds(begin, block), :],
                    w_buf.at[:, pl.ds(begin, block), pl.ds(other, lanes)],
                    sems.at[i, 1],
                ),
            )
        )
        for copy in copies[-1]:
            copy.start()
    for side in range(2):
        cut = slice(side * lanes, (side + 1) * lanes)

        def window(part):
            rows = [prev_ref[part, :, cut], proj_ref[part, :, cut], next_ref[part, :, cut]]
            return jnp.concatenate(rows, axis=0).astype(jnp.float32)

        taps = packed_ref[count:, cut]
        feat = [taps[3 * part : 3 * part + 3] for part in range(parts)]
        inner_taps = taps[9:]
        query = causal(window(0), feat[0])
        key = causal(window(1), feat[1])
        value = causal(window(2), feat[2])
        inner = causal(key * value, inner_taps)
        gated_ref[:, cut] = (query * inner)[HALO:last].astype(gated_ref.dtype)
        grad_next = next_ref[parts, :, cut].astype(jnp.float32)
        grad = jnp.concatenate([jnp.zeros_like(grad_next), packed_ref[:count, cut], grad_next], axis=0)
        mixed = adjoint(grad * query, inner_taps)
        back[0, :, cut] = adjoint(grad * inner, feat[0])[HALO:last].astype(back.dtype)
        back[1, :, cut] = adjoint(mixed * value, feat[1])[HALO:last].astype(back.dtype)
        back[2, :, cut] = adjoint(mixed * key, feat[2])[HALO:last].astype(back.dtype)
    contract = (((1,), (1,)), ((), ()))
    leaving = []
    for i in range(steps):
        for copy in copies[i]:
            copy.wait()
        cut = slice(i * block, (i + 1) * block)
        total = lax.dot_general(back[0], w_buf[0, cut], contract, preferred_element_type=jnp.float32)
        for part in range(1, parts):
            total = total + lax.dot_general(
                back[part], w_buf[part, cut], contract, preferred_element_type=jnp.float32
            )
        o_buf[:, cut] = total.astype(o_buf.dtype)
        leaving.append(pltpu.make_async_copy(o_buf.at[:, cut], o_ref.at[:, cut], sems.at[i, 2]))
        leaving[-1].start()
    for copy in leaving:
        copy.wait()


def mix(upper, proj, prev, following, packed, mine, theirs):
    parts, depth, lanes = mine.shape
    count = proj.shape[1]
    steps = 8
    return pl.pallas_call(
        mix_kernel,
        in_specs=[smem()] + [vmem()] * 4 + [hbm()] * 2,
        out_specs=[vmem(), hbm()],
        out_shape=[
            jax.ShapeDtypeStruct((count, 2 * lanes), jnp.bfloat16),
            jax.ShapeDtypeStruct((count, depth), jnp.bfloat16),
        ],
        scratch_shapes=[
            pltpu.VMEM((parts, depth, 2 * lanes), mine.dtype),
            pltpu.VMEM((parts, count, 2 * lanes), jnp.bfloat16),
            pltpu.VMEM((count, depth), jnp.bfloat16),
            pltpu.SemaphoreType.DMA((steps, 3)),
        ],
        compiler_params=PARAMS,
        name="mix",
    )(upper, proj, prev, following, packed, mine, theirs)


def encode(tokens):
    wide = tokens.astype(jnp.float32)
    peak = jnp.max(jnp.abs(wide), axis=1, keepdims=True)
    power = jnp.clip(jnp.floor(jnp.log2(jnp.maximum(peak, 1e-37))), -110.0, 110.0)
    scaled = wide * jnp.exp2(TOP - power)
    return jnp.concatenate(
        [scaled, jnp.broadcast_to(power, (tokens.shape[0], 128))], axis=1
    ).astype(jnp.float16)


def build(sizes):
    ring = sizes[0] * 2

    strips = sizes[0] * sizes[1] * 4

    def along(value, step):
        def route(yh, x, c, yl):
            strip = ((yh * sizes[1] + x) * 2 + yl) * 2 + c + step
            if not 0 <= strip < strips:
                return None
            return (strip // 4 // sizes[1], strip // 4 % sizes[1], strip % 2, strip // 2 % 2)

        return exchange(value, ("yh", "x", "c", "yl"), (sizes[0], sizes[1], 2, 2), route)

    def local(tokens, proj_weight, feat_taps, inner_taps, grad_out):
        upper = lax.axis_index("yl")
        core = lax.axis_index("c")
        channels = inner_taps.shape[1]
        flag = upper.astype(jnp.int32).reshape(1)

        count = grad_out.shape[0] // 2
        taps = jnp.concatenate([feat_taps.reshape(9, channels), inner_taps], axis=0)

        def message(which):
            rows = lax.dynamic_slice_in_dim(grad_out, which * count, count, 0)
            return jnp.concatenate([rows.astype(jnp.float32), taps], axis=0)

        near = swap_homes(message(upper))
        far = exchange(message(1 - upper), ("c", "yl"), (2, 2), lambda c, yl: (1 - yl, c))
        planes = proj_weight.transpose(1, 0, 2)
        rehomed = swap_homes(encode(tokens))
        rehomed, near, far, sent = lax.optimization_barrier((rehomed, near, far, planes))

        def beside(yh, c, yl):
            place = (yh * 2 + yl + (1 if c else ring - 1)) % ring
            return (place // 2, c, place % 2)

        theirs = exchange(sent, ("yh", "c", "yl"), (sizes[0], 2, 2), beside)
        gathered = lax.all_gather(rehomed, "z", axis=0, tiled=True).astype(jnp.bfloat16)
        packed = jnp.where(
            core == 0,
            jnp.concatenate([near, far], axis=1),
            jnp.concatenate([far, near], axis=1),
        )

        proj, head, tail = project(flag, gathered, packed, planes, theirs)
        prev = along(tail, 1)
        following = along(head, -1)
        gated, spread = mix(flag, proj, prev, following, packed, planes, theirs)
        grad_tokens = lax.psum_scatter(spread, "z", scatter_dimension=0, tiled=True)

        first, second = gated[:, :channels], gated[:, channels:]
        near = swap_homes(jnp.where(core == 0, first, second))
        far = exchange(
            jnp.where(core == 0, second, first), ("c", "yl"), (2, 2), lambda c, yl: (yl, 1 - c)
        )
        gated = jnp.where(
            upper == 0,
            jnp.concatenate([near, far], axis=0),
            jnp.concatenate([far, near], axis=0),
        )
        grad_tokens, gated = lax.optimization_barrier((grad_tokens, gated))
        return (gated, swap_homes(grad_tokens))

    return local


def solution(mesh):
    sizes = (4, 4, 2, 2, 12)
    grid = Mesh(mesh.devices.reshape(sizes), CTX + TP)
    in_specs = (
        P(CTX + TP, None),
        P(None, None, TP),
        P(None, None, TP),
        P(None, TP),
        P(CTX, TP),
    )
    out_specs = (P(CTX, TP), P(CTX + TP, None))
    return jax.shard_map(build(sizes), mesh=grid, in_specs=in_specs, out_specs=out_specs, check_vma=False)
```

```python
import jax
import jax.numpy as jnp
from jax import lax
from jax.experimental import pallas as pl
from jax.experimental.pallas import tpu as pltpu
from jax.sharding import Mesh
from jax.sharding import PartitionSpec as P

CTX = ("yh", "x", "c")
TP = ("yl", "z")
HALO = 8
TOP = 13.0


def exchange(value, axes, sizes, route):
    total = 1
    for size in sizes:
        total *= size
    pairs = []
    for source in range(total):
        coords, rest = [], source
        for size in reversed(sizes):
            coords.append(rest % size)
            rest //= size
        target = route(*reversed(coords))
        if target is None:
            continue
        flat = 0
        for place, size in zip(target, sizes):
            flat = flat * size + place
        pairs.append((source, flat))
    return lax.ppermute(value, axes, pairs)


def swap_homes(value):
    return exchange(value, ("c", "yl"), (2, 2), lambda c, yl: (yl, c))


def vmem():
    return pl.BlockSpec(memory_space=pltpu.MemorySpace.VMEM)


def smem():
    return pl.BlockSpec(memory_space=pltpu.MemorySpace.SMEM)


def hbm():
    return pl.BlockSpec(memory_space=pltpu.MemorySpace.HBM)


PARAMS = pltpu.CompilerParams(vmem_limit_bytes=24 * 1024 * 1024)


def slots(upper_ref, lanes):
    upper = upper_ref[0]
    return pl.multiple_of(upper * lanes, lanes), pl.multiple_of((1 - upper) * lanes, lanes)


def side_by_side(mine_ref, theirs_ref, part, cut):
    return jnp.concatenate([mine_ref[part, cut], theirs_ref[part, cut]], axis=1)


def project_kernel(upper_ref, x_ref, packed_ref, mine_ref, theirs_ref, o_ref, head_ref, tail_ref):
    parts, depth, lanes = mine_ref.shape
    count = x_ref.shape[0]
    own, other = slots(upper_ref, lanes)
    scale = jnp.exp2(x_ref[:, depth : depth + 1].astype(jnp.float32) - TOP)
    block = min(depth, 1024)
    for j in range(parts):
        total = None
        for begin in range(0, depth, block):
            cut = slice(begin, begin + block)
            piece = jnp.dot(
                x_ref[:, cut],
                side_by_side(mine_ref, theirs_ref, j, cut),
                preferred_element_type=jnp.float32,
            )
            total = piece if total is None else total + piece
        total = total * scale
        for place, half in ((own, total[:, :lanes]), (other, total[:, lanes:])):
            spot = pl.ds(place, lanes)
            o_ref[j, :, spot] = half.astype(o_ref.dtype)
            head_ref[j, :, spot] = half[:HALO].astype(head_ref.dtype)
            tail_ref[j, :, spot] = half[count - HALO :].astype(tail_ref.dtype)
    head_ref[parts] = packed_ref[:HALO].astype(head_ref.dtype)


def project(upper, rows, packed, mine, theirs):
    parts, _, lanes = mine.shape
    count = rows.shape[0]
    return pl.pallas_call(
        project_kernel,
        in_specs=[smem()] + [vmem()] * 4,
        out_specs=[vmem()] * 3,
        out_shape=[
            jax.ShapeDtypeStruct((parts, count, 2 * lanes), jnp.bfloat16),
            jax.ShapeDtypeStruct((parts + 1, HALO, 2 * lanes), jnp.bfloat16),
            jax.ShapeDtypeStruct((parts, HALO, 2 * lanes), jnp.bfloat16),
        ],
        compiler_params=PARAMS,
        name="project",
    )(upper, rows, packed, mine, theirs)


def causal(series, taps):
    total = taps[0:1] * series
    for offset in range(1, taps.shape[0]):
        total = total + taps[offset : offset + 1] * pltpu.roll(series, offset, 0)
    return total


def adjoint(series, taps):
    total = taps[0:1] * series
    for offset in range(1, taps.shape[0]):
        total = total + taps[offset : offset + 1] * pltpu.roll(series, series.shape[0] - offset, 0)
    return total


def mix_kernel(
    upper_ref, proj_ref, prev_ref, next_ref, packed_ref, mine_ref, theirs_ref,
    gated_ref, o_ref, back, o_buf, sems,
):
    parts, depth, lanes = mine_ref.shape
    count = proj_ref.shape[1]
    last = HALO + count
    steps = sems.shape[0]
    block = depth // steps
    own, other = slots(upper_ref, lanes)
    for side in range(2):
        cut = slice(side * lanes, (side + 1) * lanes)

        def window(part):
            rows = [prev_ref[part, :, cut], proj_ref[part, :, cut], next_ref[part, :, cut]]
            return jnp.concatenate(rows, axis=0).astype(jnp.float32)

        taps = packed_ref[count:, cut]
        feat = [taps[3 * part : 3 * part + 3] for part in range(parts)]
        inner_taps = taps[9:]
        query = causal(window(0), feat[0])
        key = causal(window(1), feat[1])
        value = causal(window(2), feat[2])
        inner = causal(key * value, inner_taps)
        gated_ref[:, cut] = (query * inner)[HALO:last].astype(gated_ref.dtype)
        grad_next = next_ref[parts, :, cut].astype(jnp.float32)
        grad = jnp.concatenate([jnp.zeros_like(grad_next), packed_ref[:count, cut], grad_next], axis=0)
        mixed = adjoint(grad * query, inner_taps)
        back[0, :, cut] = adjoint(grad * inner, feat[0])[HALO:last].astype(back.dtype)
        back[1, :, cut] = adjoint(mixed * value, feat[1])[HALO:last].astype(back.dtype)
        back[2, :, cut] = adjoint(mixed * key, feat[2])[HALO:last].astype(back.dtype)
    left = [
        jnp.concatenate([back[part, :, pl.ds(own, lanes)], back[part, :, pl.ds(other, lanes)]], axis=1)
        for part in range(parts)
    ]
    contract = (((1,), (1,)), ((), ()))
    leaving = []
    for i in range(steps):
        cut = slice(i * block, (i + 1) * block)
        total = None
        for part in range(parts):
            piece = lax.dot_general(
                left[part],
                side_by_side(mine_ref, theirs_ref, part, cut),
                contract,
                preferred_element_type=jnp.float32,
            )
            total = piece if total is None else total + piece
        o_buf[:, cut] = total.astype(o_buf.dtype)
        leaving.append(pltpu.make_async_copy(o_buf.at[:, cut], o_ref.at[:, cut], sems.at[i]))
        leaving[-1].start()
    for copy in leaving:
        copy.wait()


def mix(upper, proj, prev, following, packed, mine, theirs):
    parts, depth, lanes = mine.shape
    count = proj.shape[1]
    steps = 8
    return pl.pallas_call(
        mix_kernel,
        in_specs=[smem()] + [vmem()] * 6,
        out_specs=[vmem(), hbm()],
        out_shape=[
            jax.ShapeDtypeStruct((count, 2 * lanes), jnp.bfloat16),
            pltpu.HBM((count, depth), jnp.bfloat16),
        ],
        scratch_shapes=[
            pltpu.VMEM((parts, count, 2 * lanes), jnp.bfloat16),
            pltpu.VMEM((count, depth), jnp.bfloat16),
            pltpu.SemaphoreType.DMA((steps,)),
        ],
        compiler_params=PARAMS,
        name="mix",
    )(upper, proj, prev, following, packed, mine, theirs)


def encode(tokens):
    wide = tokens.astype(jnp.float32)
    peak = jnp.max(jnp.abs(wide), axis=1, keepdims=True)
    power = jnp.clip(jnp.floor(jnp.log2(jnp.maximum(peak, 1e-37))), -110.0, 110.0)
    scaled = wide * jnp.exp2(TOP - power)
    return jnp.concatenate(
        [scaled, jnp.broadcast_to(power, (tokens.shape[0], 128))], axis=1
    ).astype(jnp.float16)


def build(sizes):
    ring = sizes[0] * 2

    strips = sizes[0] * sizes[1] * 4

    def along(value, step):
        def route(yh, x, c, yl):
            strip = ((yh * sizes[1] + x) * 2 + yl) * 2 + c + step
            if not 0 <= strip < strips:
                return None
            return (strip // 4 // sizes[1], strip // 4 % sizes[1], strip % 2, strip // 2 % 2)

        return exchange(value, ("yh", "x", "c", "yl"), (sizes[0], sizes[1], 2, 2), route)

    def local(tokens, proj_weight, feat_taps, inner_taps, grad_out):
        upper = lax.axis_index("yl")
        core = lax.axis_index("c")
        channels = inner_taps.shape[1]
        flag = upper.astype(jnp.int32).reshape(1)

        count = grad_out.shape[0] // 2
        taps = jnp.concatenate([feat_taps.reshape(9, channels), inner_taps], axis=0)

        def message(which):
            rows = lax.dynamic_slice_in_dim(grad_out, which * count, count, 0)
            return jnp.concatenate([rows.astype(jnp.float32), taps], axis=0)

        near, far = message(upper), message(1 - upper)
        planes = proj_weight.transpose(1, 0, 2)
        rehomed = swap_homes(encode(tokens))
        rehomed, sent, near, far = lax.optimization_barrier((rehomed, planes, near, far))
        near = swap_homes(near)
        far = exchange(far, ("c", "yl"), (2, 2), lambda c, yl: (1 - yl, c))

        def beside(yh, c, yl):
            place = (yh * 2 + yl + (1 if c else ring - 1)) % ring
            return (place // 2, c, place % 2)

        theirs = exchange(sent, ("yh", "c", "yl"), (sizes[0], 2, 2), beside)
        gathered = lax.all_gather(rehomed, "z", axis=0, tiled=True)
        gathered, near, far = lax.optimization_barrier((gathered, near, far))
        gathered = gathered.astype(jnp.bfloat16)
        packed = jnp.where(
            core == 0,
            jnp.concatenate([near, far], axis=1),
            jnp.concatenate([far, near], axis=1),
        )

        proj, head, tail = project(flag, gathered, packed, planes, theirs)
        prev = along(tail, 1)
        following = along(head, -1)
        gated, spread = mix(flag, proj, prev, following, packed, planes, theirs)
        grad_tokens = lax.psum_scatter(spread, "z", scatter_dimension=0, tiled=True)

        first, second = gated[:, :channels], gated[:, channels:]
        near = swap_homes(jnp.where(core == 0, first, second))
        far = exchange(
            jnp.where(core == 0, second, first), ("c", "yl"), (2, 2), lambda c, yl: (yl, 1 - c)
        )
        gated = jnp.where(
            upper == 0,
            jnp.concatenate([near, far], axis=0),
            jnp.concatenate([far, near], axis=0),
        )
        grad_tokens, gated = lax.optimization_barrier((grad_tokens, gated))
        return (gated, swap_homes(grad_tokens))

    return local


def solution(mesh):
    sizes = (4, 4, 2, 2, 12)
    grid = Mesh(mesh.devices.reshape(sizes), CTX + TP)
    in_specs = (
        P(CTX + TP, None),
        P(None, None, TP),
        P(None, None, TP),
        P(None, TP),
        P(CTX, TP),
    )
    out_specs = (P(CTX, TP), P(CTX + TP, None))
    return jax.shard_map(build(sizes), mesh=grid, in_specs=in_specs, out_specs=out_specs, check_vma=False)
```

```python
import jax
import jax.numpy as jnp
from jax import lax
from jax.experimental import pallas as pl
from jax.experimental.pallas import tpu as pltpu
from jax.sharding import Mesh
from jax.sharding import PartitionSpec as P

CTX = ("yh", "x", "c")
TP = ("yl", "z")
HALO = 8
TOP = 13.0


def exchange(value, axes, sizes, route):
    total = 1
    for size in sizes:
        total *= size
    pairs = []
    for source in range(total):
        coords, rest = [], source
        for size in reversed(sizes):
            coords.append(rest % size)
            rest //= size
        target = route(*reversed(coords))
        if target is None:
            continue
        flat = 0
        for place, size in zip(target, sizes):
            flat = flat * size + place
        pairs.append((source, flat))
    return lax.ppermute(value, axes, pairs)


def vmem():
    return pl.BlockSpec(memory_space=pltpu.MemorySpace.VMEM)


def smem():
    return pl.BlockSpec(memory_space=pltpu.MemorySpace.SMEM)


def hbm():
    return pl.BlockSpec(memory_space=pltpu.MemorySpace.HBM)


PARAMS = pltpu.CompilerParams(vmem_limit_bytes=24 * 1024 * 1024)


def slots(upper_ref, lanes):
    upper = upper_ref[0]
    return pl.multiple_of(upper * lanes, lanes), pl.multiple_of((1 - upper) * lanes, lanes)


def side_by_side(mine_ref, theirs_ref, part, cut):
    return jnp.concatenate([mine_ref[part, cut], theirs_ref[part, cut]], axis=1)


def message_kernel(upper_ref, grad_ref, feat_ref, inner_ref, o_ref):
    count = grad_ref.shape[0] // 2
    begin = pl.multiple_of((1 - upper_ref[0]) * count, 16)
    o_ref[:count] = grad_ref[pl.ds(begin, count)].astype(o_ref.dtype)
    for part in range(3):
        o_ref[count + 3 * part : count + 3 * part + 3] = feat_ref[part]
    o_ref[count + 9 :] = inner_ref[...]


def message(upper, grad, feat, inner):
    rows = grad.shape[0] // 2 + 9 + inner.shape[0]
    return pl.pallas_call(
        message_kernel,
        grid=(1,),
        in_specs=[smem()] + [pl.BlockSpec(v.shape, lambda i, n=v.ndim: (0,) * n) for v in (grad, feat, inner)],
        out_specs=pl.BlockSpec((rows, grad.shape[1]), lambda i: (0, 0)),
        out_shape=jax.ShapeDtypeStruct((rows, grad.shape[1]), jnp.float32),
        compiler_params=PARAMS,
        name="message",
    )(upper, grad, feat, inner)


def project_kernel(upper_ref, x_ref, grad_ref, came_ref, mine_ref, theirs_ref, o_ref, head_ref, tail_ref):
    parts, depth, lanes = mine_ref.shape
    count = x_ref.shape[0]
    own, other = slots(upper_ref, lanes)
    scale = jnp.exp2(x_ref[:, depth : depth + 1].astype(jnp.float32) - TOP)
    block = min(depth, 1024)
    for j in range(parts):
        total = None
        for begin in range(0, depth, block):
            cut = slice(begin, begin + block)
            piece = jnp.dot(
                x_ref[:, cut],
                side_by_side(mine_ref, theirs_ref, j, cut),
                preferred_element_type=jnp.float32,
            )
            total = piece if total is None else total + piece
        total = total * scale
        for place, half in ((own, total[:, :lanes]), (other, total[:, lanes:])):
            spot = pl.ds(place, lanes)
            o_ref[j, :, spot] = half.astype(o_ref.dtype)
            head_ref[j, :, spot] = half[:HALO].astype(head_ref.dtype)
            tail_ref[j, :, spot] = half[count - HALO :].astype(tail_ref.dtype)
    begin = pl.multiple_of(upper_ref[0] * count, 16)
    head_ref[parts, :, pl.ds(own, lanes)] = grad_ref[pl.ds(begin, count)][:HALO]
    head_ref[parts, :, pl.ds(other, lanes)] = came_ref[:HALO].astype(head_ref.dtype)


def project(upper, rows, grad, came, mine, theirs):
    parts, _, lanes = mine.shape
    count = rows.shape[0]
    return pl.pallas_call(
        project_kernel,
        in_specs=[smem()] + [vmem()] * 5,
        out_specs=[vmem()] * 3,
        out_shape=[
            jax.ShapeDtypeStruct((parts, count, 2 * lanes), jnp.bfloat16),
            jax.ShapeDtypeStruct((parts + 1, HALO, 2 * lanes), jnp.bfloat16),
            jax.ShapeDtypeStruct((parts, HALO, 2 * lanes), jnp.bfloat16),
        ],
        compiler_params=PARAMS,
        name="project",
    )(upper, rows, grad, came, mine, theirs)


def causal(series, taps):
    total = taps[0:1] * series
    for offset in range(1, taps.shape[0]):
        total = total + taps[offset : offset + 1] * pltpu.roll(series, offset, 0)
    return total


def adjoint(series, taps):
    total = taps[0:1] * series
    for offset in range(1, taps.shape[0]):
        total = total + taps[offset : offset + 1] * pltpu.roll(series, series.shape[0] - offset, 0)
    return total


def mix_kernel(
    upper_ref, proj_ref, prev_ref, next_ref, grad_ref, feat_ref, inner_ref, came_ref, mine_ref, theirs_ref,
    kept_ref, sent_ref, o_ref, back, o_buf, sems,
):
    parts, depth, lanes = mine_ref.shape
    count = proj_ref.shape[1]
    last = HALO + count
    steps = sems.shape[0]
    block = depth // steps
    own, other = slots(upper_ref, lanes)
    begin = pl.multiple_of(upper_ref[0] * count, 16)
    taps = came_ref[count:]
    sides = (
        (own, grad_ref[pl.ds(begin, count)], [feat_ref[part] for part in range(parts)], inner_ref[...], kept_ref),
        (other, came_ref[:count], [taps[3 * part : 3 * part + 3] for part in range(parts)], taps[9:], sent_ref),
    )
    for side, (place, here, feat, inner_taps, gated_ref) in enumerate(sides):
        spot = pl.ds(place, lanes)
        cut = slice(side * lanes, (side + 1) * lanes)

        def window(part):
            rows = [prev_ref[part, :, spot], proj_ref[part, :, spot], next_ref[part, :, spot]]
            return jnp.concatenate(rows, axis=0).astype(jnp.float32)

        query = causal(window(0), feat[0])
        key = causal(window(1), feat[1])
        value = causal(window(2), feat[2])
        inner = causal(key * value, inner_taps)
        gated_ref[...] = (query * inner)[HALO:last].astype(gated_ref.dtype)
        grad_next = next_ref[parts, :, spot].astype(jnp.float32)
        grad = jnp.concatenate([jnp.zeros_like(grad_next), here.astype(jnp.float32), grad_next], axis=0)
        mixed = adjoint(grad * query, inner_taps)
        back[0, :, cut] = adjoint(grad * inner, feat[0])[HALO:last].astype(back.dtype)
        back[1, :, cut] = adjoint(mixed * value, feat[1])[HALO:last].astype(back.dtype)
        back[2, :, cut] = adjoint(mixed * key, feat[2])[HALO:last].astype(back.dtype)
    contract = (((1,), (1,)), ((), ()))
    leaving = []
    for i in range(steps):
        cut = slice(i * block, (i + 1) * block)
        total = None
        for part in range(parts):
            piece = lax.dot_general(
                back[part],
                side_by_side(mine_ref, theirs_ref, part, cut),
                contract,
                preferred_element_type=jnp.float32,
            )
            total = piece if total is None else total + piece
        o_buf[:, cut] = total.astype(o_buf.dtype)
        leaving.append(pltpu.make_async_copy(o_buf.at[:, cut], o_ref.at[:, cut], sems.at[i]))
        leaving[-1].start()
    for copy in leaving:
        copy.wait()


def mix(upper, proj, prev, following, grad, feat, inner, came, mine, theirs):
    parts, depth, lanes = mine.shape
    count = proj.shape[1]
    steps = 8
    half = jax.ShapeDtypeStruct((count, lanes), jnp.bfloat16)
    return pl.pallas_call(
        mix_kernel,
        in_specs=[smem()] + [vmem()] * 9,
        out_specs=[vmem(), vmem(), hbm()],
        out_shape=[half, half, pltpu.HBM((count, depth), jnp.bfloat16)],
        scratch_shapes=[
            pltpu.VMEM((parts, count, 2 * lanes), jnp.bfloat16),
            pltpu.VMEM((count, depth), jnp.bfloat16),
            pltpu.SemaphoreType.DMA((steps,)),
        ],
        compiler_params=PARAMS,
        name="mix",
    )(upper, proj, prev, following, grad, feat, inner, came, mine, theirs)


def encode(tokens):
    wide = tokens.astype(jnp.float32)
    peak = jnp.max(jnp.abs(wide), axis=1, keepdims=True)
    power = jnp.clip(jnp.floor(jnp.log2(jnp.maximum(peak, 1e-37))), -110.0, 110.0)
    scaled = wide * jnp.exp2(TOP - power)
    return jnp.concatenate(
        [scaled, jnp.broadcast_to(power, (tokens.shape[0], 128))], axis=1
    ).astype(jnp.float16)


def build(sizes):
    ring = sizes[0] * 2

    strips = sizes[0] * sizes[1] * 4

    def along(value, step):
        def route(yh, x, c, yl):
            strip = ((yh * sizes[1] + x) * 2 + c) * 2 + yl + step
            if not 0 <= strip < strips:
                return None
            return (strip // 4 // sizes[1], strip // 4 % sizes[1], strip // 2 % 2, strip % 2)

        return exchange(value, ("yh", "x", "c", "yl"), (sizes[0], sizes[1], 2, 2), route)

    def across(value):
        return lax.ppermute(value, "yl", [(0, 1), (1, 0)])

    def local(tokens, proj_weight, feat_taps, inner_taps, grad_out):
        upper = lax.axis_index("yl")
        flag = upper.astype(jnp.int32).reshape(1)

        note = message(flag, grad_out, feat_taps, inner_taps)
        planes = proj_weight.transpose(1, 0, 2)
        rows, sent, note = lax.optimization_barrier((encode(tokens), planes, note))
        came = across(note)

        def beside(yh, c, yl):
            place = (yh * 2 + yl + (1 if c else ring - 1)) % ring
            return (place // 2, c, place % 2)

        theirs = exchange(sent, ("yh", "c", "yl"), (sizes[0], 2, 2), beside)
        gathered = lax.all_gather(rows, "z", axis=0, tiled=True)
        gathered, came = lax.optimization_barrier((gathered, came))
        gathered = gathered.astype(jnp.bfloat16)

        proj, head, tail = project(flag, gathered, grad_out, came, planes, theirs)
        prev = along(tail, 1)
        following = along(head, -1)
        kept, leaving, spread = mix(
            flag, proj, prev, following, grad_out, feat_taps, inner_taps, came, planes, theirs
        )
        grad_tokens = lax.psum_scatter(spread, "z", scatter_dimension=0, tiled=True)
        arrived = across(leaving)
        gated = jnp.where(
            upper == 0,
            jnp.concatenate([kept, arrived], axis=0),
            jnp.concatenate([arrived, kept], axis=0),
        )
        return (gated, grad_tokens)

    return local


def solution(mesh):
    sizes = (4, 4, 2, 2, 12)
    grid = Mesh(mesh.devices.reshape(sizes), CTX + TP)
    in_specs = (
        P(CTX + TP, None),
        P(None, None, TP),
        P(None, None, TP),
        P(None, TP),
        P(CTX, TP),
    )
    out_specs = (P(CTX, TP), P(CTX + TP, None))
    return jax.shard_map(build(sizes), mesh=grid, in_specs=in_specs, out_specs=out_specs, check_vma=False)
```

```python
import jax
import jax.numpy as jnp
from jax import lax
from jax.experimental import pallas as pl
from jax.experimental.pallas import tpu as pltpu
from jax.sharding import Mesh
from jax.sharding import PartitionSpec as P

CTX = ("yh", "x", "c")
TP = ("yl", "z")
HALO = 8
TOP = 13.0
SHARD = 24
FOLD = 16


def exchange(value, axes, sizes, route):
    total = 1
    for size in sizes:
        total *= size
    pairs = []
    for source in range(total):
        coords, rest = [], source
        for size in reversed(sizes):
            coords.append(rest % size)
            rest //= size
        target = route(*reversed(coords))
        if target is None:
            continue
        flat = 0
        for place, size in zip(target, sizes):
            flat = flat * size + place
        pairs.append((source, flat))
    return lax.ppermute(value, axes, pairs)


def vmem():
    return pl.BlockSpec(memory_space=pltpu.MemorySpace.VMEM)


def smem():
    return pl.BlockSpec(memory_space=pltpu.MemorySpace.SMEM)


def hbm():
    return pl.BlockSpec(memory_space=pltpu.MemorySpace.HBM)


PARAMS = pltpu.CompilerParams(vmem_limit_bytes=24 * 1024 * 1024)


def slots(upper_ref, lanes):
    upper = upper_ref[0]
    return pl.multiple_of(upper * lanes, lanes), pl.multiple_of((1 - upper) * lanes, lanes)


def side_by_side(mine_ref, theirs_ref, part, cut):
    return jnp.concatenate([mine_ref[part, cut], theirs_ref[part, cut]], axis=1)


def message_kernel(upper_ref, grad_ref, feat_ref, inner_ref, o_ref):
    count = grad_ref.shape[0] // 2
    begin = pl.multiple_of((1 - upper_ref[0]) * count, 16)
    o_ref[:count] = grad_ref[pl.ds(begin, count)].astype(o_ref.dtype)
    for part in range(3):
        o_ref[count + 3 * part : count + 3 * part + 3] = feat_ref[part]
    o_ref[count + 9 :] = inner_ref[...]


def message(upper, grad, feat, inner):
    rows = grad.shape[0] // 2 + 9 + inner.shape[0]
    return pl.pallas_call(
        message_kernel,
        grid=(1,),
        in_specs=[smem()] + [pl.BlockSpec(v.shape, lambda i, n=v.ndim: (0,) * n) for v in (grad, feat, inner)],
        out_specs=pl.BlockSpec((rows, grad.shape[1]), lambda i: (0, 0)),
        out_shape=jax.ShapeDtypeStruct((rows, grad.shape[1]), jnp.float32),
        compiler_params=PARAMS,
        name="message",
    )(upper, grad, feat, inner)


def project_kernel(upper_ref, x_ref, grad_ref, came_ref, mine_ref, theirs_ref, o_ref, head_ref, tail_ref):
    parts, depth, lanes = mine_ref.shape
    count = x_ref.shape[0]
    own, other = slots(upper_ref, lanes)
    scale = jnp.exp2(x_ref[:, depth : depth + 1].astype(jnp.float32) - TOP)
    block = min(depth, 1024)
    for j in range(parts):
        total = None
        for begin in range(0, depth, block):
            cut = slice(begin, begin + block)
            piece = jnp.dot(
                x_ref[:, cut],
                side_by_side(mine_ref, theirs_ref, j, cut),
                preferred_element_type=jnp.float32,
            )
            total = piece if total is None else total + piece
        total = total * scale
        for place, half in ((own, total[:, :lanes]), (other, total[:, lanes:])):
            spot = pl.ds(place, lanes)
            o_ref[j, :, spot] = half.astype(o_ref.dtype)
            head_ref[j, :, spot] = half[:HALO].astype(head_ref.dtype)
            tail_ref[j, :, spot] = half[count - HALO :].astype(tail_ref.dtype)
    begin = pl.multiple_of(upper_ref[0] * count, 16)
    head_ref[parts, :, pl.ds(own, lanes)] = grad_ref[pl.ds(begin, count)][:HALO]
    head_ref[parts, :, pl.ds(other, lanes)] = came_ref[:HALO].astype(head_ref.dtype)


def project(upper, rows, grad, came, mine, theirs):
    parts, _, lanes = mine.shape
    count = rows.shape[0]
    return pl.pallas_call(
        project_kernel,
        in_specs=[smem()] + [vmem()] * 5,
        out_specs=[vmem()] * 3,
        out_shape=[
            jax.ShapeDtypeStruct((parts, count, 2 * lanes), jnp.bfloat16),
            jax.ShapeDtypeStruct((parts + 1, HALO, 2 * lanes), jnp.bfloat16),
            jax.ShapeDtypeStruct((parts, HALO, 2 * lanes), jnp.bfloat16),
        ],
        compiler_params=PARAMS,
        name="project",
    )(upper, rows, grad, came, mine, theirs)


def causal(series, taps):
    total = taps[0:1] * series
    for offset in range(1, taps.shape[0]):
        total = total + taps[offset : offset + 1] * pltpu.roll(series, offset, 0)
    return total


def adjoint(series, taps):
    total = taps[0:1] * series
    for offset in range(1, taps.shape[0]):
        total = total + taps[offset : offset + 1] * pltpu.roll(series, series.shape[0] - offset, 0)
    return total


def mix_kernel(
    upper_ref, proj_ref, prev_ref, next_ref, grad_ref, feat_ref, inner_ref, came_ref, mine_ref, theirs_ref,
    kept_ref, sent_ref, o_ref, back, extra, o_buf, sems,
):
    parts, depth, lanes = mine_ref.shape
    count = proj_ref.shape[1]
    last = HALO + count
    block = depth // 8
    own, other = slots(upper_ref, lanes)
    begin = pl.multiple_of(upper_ref[0] * count, 16)
    shards = count // SHARD
    body = SHARD - 1
    main = shards * body
    taps = came_ref[count:]
    sides = (
        (own, grad_ref[pl.ds(begin, count)], [feat_ref[part] for part in range(parts)], inner_ref[...], kept_ref),
        (other, came_ref[:count], [taps[3 * part : 3 * part + 3] for part in range(parts)], taps[9:], sent_ref),
    )
    for side, (place, here, feat, inner_taps, gated_ref) in enumerate(sides):
        spot = pl.ds(place, lanes)
        cut = slice(side * lanes, (side + 1) * lanes)

        def window(part):
            rows = [prev_ref[part, :, spot], proj_ref[part, :, spot], next_ref[part, :, spot]]
            return jnp.concatenate(rows, axis=0).astype(jnp.float32)

        query = causal(window(0), feat[0])
        key = causal(window(1), feat[1])
        value = causal(window(2), feat[2])
        inner = causal(key * value, inner_taps)
        gated_ref[...] = (query * inner)[HALO:last].astype(gated_ref.dtype)
        grad_next = next_ref[parts, :, spot].astype(jnp.float32)
        grad = jnp.concatenate([jnp.zeros_like(grad_next), here.astype(jnp.float32), grad_next], axis=0)
        mixed = adjoint(grad * query, inner_taps)
        for part, series in enumerate((grad * inner, mixed * value, mixed * key)):
            rows = adjoint(series, feat[part])[HALO:last]
            for k in range(shards):
                first = k * SHARD
                back[part, k * body : (k + 1) * body, cut] = rows[first : first + body]
                back[part, main + k : main + k + 1, cut] = rows[first + body : first + SHARD]
    left = [back[part].astype(jnp.bfloat16) for part in range(parts)]
    contract = (((1,), (1,)), ((), ()))
    extra[...] = jnp.zeros_like(extra)
    leaving = []
    wide = depth // FOLD
    for i in range(depth // block):
        cut = slice(i * block, (i + 1) * block)
        total = None
        for part in range(parts):
            piece = lax.dot_general(
                left[part],
                side_by_side(mine_ref, theirs_ref, part, cut),
                contract,
                preferred_element_type=jnp.float32,
            )
            total = piece if total is None else total + piece
        o_buf[:, cut] = total[:main].astype(o_buf.dtype)
        leaving.append(pltpu.make_async_copy(o_buf.at[:, cut], o_ref.at[:, cut], sems.at[i]))
        leaving[-1].start()
        for k in range(shards):
            for fold in range(block // wide):
                line = k * body + i * (block // wide) + fold
                extra[line : line + 1] = total[main + k : main + k + 1, fold * wide : (fold + 1) * wide]
    o_buf[:, depth:] = extra[...].astype(o_buf.dtype)
    leaving.append(pltpu.make_async_copy(o_buf.at[:, depth:], o_ref.at[:, depth:], sems.at[8]))
    leaving[-1].start()
    for copy in leaving:
        copy.wait()


def mix(upper, proj, prev, following, grad, feat, inner, came, mine, theirs):
    parts, depth, lanes = mine.shape
    count = proj.shape[1]
    half = jax.ShapeDtypeStruct((count, lanes), jnp.bfloat16)
    main = count // SHARD * (SHARD - 1)
    return pl.pallas_call(
        mix_kernel,
        in_specs=[smem()] + [vmem()] * 9,
        out_specs=[vmem(), vmem(), hbm()],
        out_shape=[half, half, pltpu.HBM((main, depth + depth // FOLD), jnp.bfloat16)],
        scratch_shapes=[
            pltpu.VMEM((parts, count, 2 * lanes), jnp.float32),
            pltpu.VMEM((main, depth // FOLD), jnp.float32),
            pltpu.VMEM((main, depth + depth // FOLD), jnp.bfloat16),
            pltpu.SemaphoreType.DMA((9,)),
        ],
        compiler_params=PARAMS,
        name="mix",
    )(upper, proj, prev, following, grad, feat, inner, came, mine, theirs)


def encode(tokens):
    wide = tokens.astype(jnp.float32)
    peak = jnp.max(jnp.abs(wide), axis=1, keepdims=True)
    power = jnp.clip(jnp.floor(jnp.log2(jnp.maximum(peak, 1e-37))), -110.0, 110.0)
    scaled = wide * jnp.exp2(TOP - power)
    return jnp.concatenate(
        [scaled, jnp.broadcast_to(power, (tokens.shape[0], 128))], axis=1
    ).astype(jnp.float16)


def build(sizes):
    ring = sizes[0] * 2

    strips = sizes[0] * sizes[1] * 4

    def along(value, step):
        def route(yh, x, c, yl):
            strip = ((yh * sizes[1] + x) * 2 + c) * 2 + yl + step
            if not 0 <= strip < strips:
                return None
            return (strip // 4 // sizes[1], strip // 4 % sizes[1], strip // 2 % 2, strip % 2)

        return exchange(value, ("yh", "x", "c", "yl"), (sizes[0], sizes[1], 2, 2), route)

    def across(value):
        return lax.ppermute(value, "yl", [(0, 1), (1, 0)])

    def local(tokens, proj_weight, feat_taps, inner_taps, grad_out):
        upper = lax.axis_index("yl")
        flag = upper.astype(jnp.int32).reshape(1)

        note = message(flag, grad_out, feat_taps, inner_taps)
        planes = proj_weight.transpose(1, 0, 2)
        rows, sent, note = lax.optimization_barrier((encode(tokens), planes, note))
        came = across(note)

        def beside(yh, c, yl):
            place = (yh * 2 + yl + (1 if c else ring - 1)) % ring
            return (place // 2, c, place % 2)

        theirs = exchange(sent, ("yh", "c", "yl"), (sizes[0], 2, 2), beside)
        gathered = lax.all_gather(rows, "z", axis=0, tiled=True)
        gathered, came = lax.optimization_barrier((gathered, came))
        gathered = gathered.astype(jnp.bfloat16)

        proj, head, tail = project(flag, gathered, grad_out, came, planes, theirs)
        prev = along(tail, 1)
        following = along(head, -1)
        kept, leaving, spread = mix(
            flag, proj, prev, following, grad_out, feat_taps, inner_taps, came, planes, theirs
        )
        arrived = across(leaving)
        summed = lax.psum_scatter(spread, "z", scatter_dimension=0, tiled=True)
        summed = lax.optimization_barrier(summed)
        depth = tokens.shape[1]
        grad_tokens = jnp.concatenate(
            [summed[:, :depth], summed[:FOLD, depth:].reshape(1, depth)], axis=0
        )
        gated = jnp.where(
            upper == 0,
            jnp.concatenate([kept, arrived], axis=0),
            jnp.concatenate([arrived, kept], axis=0),
        )
        return (gated, grad_tokens)

    return local


def solution(mesh):
    sizes = (4, 4, 2, 2, 12)
    grid = Mesh(mesh.devices.reshape(sizes), CTX + TP)
    in_specs = (
        P(CTX + TP, None),
        P(None, None, TP),
        P(None, None, TP),
        P(None, TP),
        P(CTX, TP),
    )
    out_specs = (P(CTX, TP), P(CTX + TP, None))
    return jax.shard_map(build(sizes), mesh=grid, in_specs=in_specs, out_specs=out_specs, check_vma=False)
```

```python
import jax
import jax.numpy as jnp
from jax import lax
from jax.experimental import pallas as pl
from jax.experimental.pallas import tpu as pltpu
from jax.sharding import Mesh
from jax.sharding import PartitionSpec as P

CTX = ("yh", "x", "c")
TP = ("yl", "z")
HALO = 8
TOP = 13.0
SHARD = 24
FOLD = 16


def exchange(value, axes, sizes, route):
    total = 1
    for size in sizes:
        total *= size
    pairs = []
    for source in range(total):
        coords, rest = [], source
        for size in reversed(sizes):
            coords.append(rest % size)
            rest //= size
        target = route(*reversed(coords))
        if target is None:
            continue
        flat = 0
        for place, size in zip(target, sizes):
            flat = flat * size + place
        pairs.append((source, flat))
    return lax.ppermute(value, axes, pairs)


def vmem():
    return pl.BlockSpec(memory_space=pltpu.MemorySpace.VMEM)


def smem():
    return pl.BlockSpec(memory_space=pltpu.MemorySpace.SMEM)


def hbm():
    return pl.BlockSpec(memory_space=pltpu.MemorySpace.HBM)


PARAMS = pltpu.CompilerParams(vmem_limit_bytes=24 * 1024 * 1024)


def slots(upper_ref, lanes):
    upper = upper_ref[0]
    return pl.multiple_of(upper * lanes, lanes), pl.multiple_of((1 - upper) * lanes, lanes)


def side_by_side(mine_ref, theirs_ref, part, cut):
    return jnp.concatenate([mine_ref[part, cut], theirs_ref[part, cut]], axis=1)


def message_kernel(upper_ref, grad_ref, feat_ref, inner_ref, o_ref):
    count = grad_ref.shape[0] // 2
    begin = pl.multiple_of((1 - upper_ref[0]) * count, 16)
    o_ref[:count] = grad_ref[pl.ds(begin, count)].astype(o_ref.dtype)
    for part in range(3):
        o_ref[count + 3 * part : count + 3 * part + 3] = feat_ref[part]
    o_ref[count + 9 :] = inner_ref[...]


def message(upper, grad, feat, inner):
    rows = grad.shape[0] // 2 + 9 + inner.shape[0]
    return pl.pallas_call(
        message_kernel,
        grid=(1,),
        in_specs=[smem()] + [pl.BlockSpec(v.shape, lambda i, n=v.ndim: (0,) * n) for v in (grad, feat, inner)],
        out_specs=pl.BlockSpec((rows, grad.shape[1]), lambda i: (0, 0)),
        out_shape=jax.ShapeDtypeStruct((rows, grad.shape[1]), jnp.float32),
        compiler_params=PARAMS,
        name="message",
    )(upper, grad, feat, inner)


def project_kernel(upper_ref, x_ref, grad_ref, came_ref, mine_ref, theirs_ref, o_ref, head_ref, tail_ref):
    parts, depth, lanes = mine_ref.shape
    count = x_ref.shape[0]
    own, other = slots(upper_ref, lanes)
    scale = jnp.exp2(x_ref[:, depth : depth + 1].astype(jnp.float32) - TOP)
    block = min(depth, 1024)
    for j in range(parts):
        total = None
        for begin in range(0, depth, block):
            cut = slice(begin, begin + block)
            piece = jnp.dot(
                x_ref[:, cut],
                side_by_side(mine_ref, theirs_ref, j, cut),
                preferred_element_type=jnp.float32,
            )
            total = piece if total is None else total + piece
        total = total * scale
        for place, half in ((own, total[:, :lanes]), (other, total[:, lanes:])):
            spot = pl.ds(place, lanes)
            o_ref[j, :, spot] = half.astype(o_ref.dtype)
            head_ref[j, :, spot] = half[:HALO].astype(head_ref.dtype)
            tail_ref[j, :, spot] = half[count - HALO :].astype(tail_ref.dtype)
    begin = pl.multiple_of(upper_ref[0] * count, 16)
    head_ref[parts, :, pl.ds(own, lanes)] = grad_ref[pl.ds(begin, count)][:HALO]
    head_ref[parts, :, pl.ds(other, lanes)] = came_ref[:HALO].astype(head_ref.dtype)


def project(upper, rows, grad, came, mine, theirs):
    parts, _, lanes = mine.shape
    count = rows.shape[0]
    return pl.pallas_call(
        project_kernel,
        in_specs=[smem()] + [vmem()] * 5,
        out_specs=[vmem()] * 3,
        out_shape=[
            jax.ShapeDtypeStruct((parts, count, 2 * lanes), jnp.bfloat16),
            jax.ShapeDtypeStruct((parts + 1, HALO, 2 * lanes), jnp.bfloat16),
            jax.ShapeDtypeStruct((parts, HALO, 2 * lanes), jnp.bfloat16),
        ],
        compiler_params=PARAMS,
        name="project",
    )(upper, rows, grad, came, mine, theirs)


def causal(series, taps):
    total = taps[0:1] * series
    for offset in range(1, taps.shape[0]):
        total = total + taps[offset : offset + 1] * pltpu.roll(series, offset, 0)
    return total


def adjoint(series, taps):
    total = taps[0:1] * series
    for offset in range(1, taps.shape[0]):
        total = total + taps[offset : offset + 1] * pltpu.roll(series, series.shape[0] - offset, 0)
    return total


def mix_kernel(
    upper_ref, proj_ref, prev_ref, next_ref, grad_ref, feat_ref, inner_ref, came_ref, mine_ref, theirs_ref,
    kept_ref, sent_ref, o_ref, back, extra, o_buf, sems,
):
    parts, depth, lanes = mine_ref.shape
    count = proj_ref.shape[1]
    last = HALO + count
    block = depth // 8
    own, other = slots(upper_ref, lanes)
    begin = pl.multiple_of(upper_ref[0] * count, 16)
    shards = count // SHARD
    body = SHARD - 1
    main = shards * body
    taps = came_ref[count:]
    sides = (
        (own, grad_ref[pl.ds(begin, count)], [feat_ref[part] for part in range(parts)], inner_ref[...], kept_ref),
        (other, came_ref[:count], [taps[3 * part : 3 * part + 3] for part in range(parts)], taps[9:], sent_ref),
    )
    for side, (place, here, feat, inner_taps, gated_ref) in enumerate(sides):
        spot = pl.ds(place, lanes)
        cut = slice(side * lanes, (side + 1) * lanes)

        def window(part):
            rows = [prev_ref[part, :, spot], proj_ref[part, :, spot], next_ref[part, :, spot]]
            return jnp.concatenate(rows, axis=0).astype(jnp.float32)

        query = causal(window(0), feat[0])
        key = causal(window(1), feat[1])
        value = causal(window(2), feat[2])
        inner = causal(key * value, inner_taps)
        gated_ref[...] = (query * inner)[HALO:last].astype(gated_ref.dtype)
        grad_next = next_ref[parts, :, spot].astype(jnp.float32)
        grad = jnp.concatenate([jnp.zeros_like(grad_next), here.astype(jnp.float32), grad_next], axis=0)
        mixed = adjoint(grad * query, inner_taps)
        for part, series in enumerate((grad * inner, mixed * value, mixed * key)):
            rows = adjoint(series, feat[part])[HALO:last]
            for k in range(shards):
                first = k * SHARD
                back[part, k * body : (k + 1) * body, cut] = rows[first : first + body]
                back[part, main + k : main + k + 1, cut] = rows[first + body : first + SHARD]
    left = [back[part].astype(jnp.bfloat16) for part in range(parts)]
    contract = (((1,), (1,)), ((), ()))
    extra[...] = jnp.zeros_like(extra)
    leaving = []
    wide = depth // FOLD
    for i in range(depth // block):
        cut = slice(i * block, (i + 1) * block)
        total = None
        for part in range(parts):
            piece = lax.dot_general(
                left[part],
                side_by_side(mine_ref, theirs_ref, part, cut),
                contract,
                preferred_element_type=jnp.float32,
            )
            total = piece if total is None else total + piece
        o_buf[:, cut] = total[:main].astype(o_buf.dtype)
        leaving.append(pltpu.make_async_copy(o_buf.at[:, cut], o_ref.at[:, cut], sems.at[i]))
        leaving[-1].start()
        for k in range(shards):
            for fold in range(block // wide):
                line = k * body + i * (block // wide) + fold
                extra[line : line + 1] = total[main + k : main + k + 1, fold * wide : (fold + 1) * wide]
    o_buf[:, depth:] = extra[...].astype(o_buf.dtype)
    leaving.append(pltpu.make_async_copy(o_buf.at[:, depth:], o_ref.at[:, depth:], sems.at[8]))
    leaving[-1].start()
    for copy in leaving:
        copy.wait()


def mix(upper, proj, prev, following, grad, feat, inner, came, mine, theirs):
    parts, depth, lanes = mine.shape
    count = proj.shape[1]
    half = jax.ShapeDtypeStruct((count, lanes), jnp.bfloat16)
    main = count // SHARD * (SHARD - 1)
    return pl.pallas_call(
        mix_kernel,
        in_specs=[smem()] + [vmem()] * 9,
        out_specs=[vmem(), vmem(), hbm()],
        out_shape=[half, half, pltpu.HBM((main, depth + depth // FOLD), jnp.bfloat16)],
        scratch_shapes=[
            pltpu.VMEM((parts, count, 2 * lanes), jnp.float32),
            pltpu.VMEM((main, depth // FOLD), jnp.float32),
            pltpu.VMEM((main, depth + depth // FOLD), jnp.bfloat16),
            pltpu.SemaphoreType.DMA((9,)),
        ],
        compiler_params=PARAMS,
        name="mix",
    )(upper, proj, prev, following, grad, feat, inner, came, mine, theirs)


def halves_kernel(upper_ref, kept_ref, arrived_ref, o_ref):
    count = kept_ref.shape[0]
    upper = upper_ref[0]
    o_ref[pl.ds(pl.multiple_of(upper * count, 16), count)] = kept_ref[...]
    o_ref[pl.ds(pl.multiple_of((1 - upper) * count, 16), count)] = arrived_ref[...]


def gather_halves(upper, kept, arrived):
    count, lanes = kept.shape
    return pl.pallas_call(
        halves_kernel,
        in_specs=[smem(), vmem(), vmem()],
        out_specs=vmem(),
        out_shape=jax.ShapeDtypeStruct((2 * count, lanes), kept.dtype),
        compiler_params=PARAMS,
        name="halves",
    )(upper, kept, arrived)


def encode(tokens):
    wide = tokens.astype(jnp.float32)
    peak = jnp.max(jnp.abs(wide), axis=1, keepdims=True)
    power = jnp.clip(jnp.floor(jnp.log2(jnp.maximum(peak, 1e-37))), -110.0, 110.0)
    scaled = wide * jnp.exp2(TOP - power)
    return jnp.concatenate(
        [scaled, jnp.broadcast_to(power, (tokens.shape[0], 128))], axis=1
    ).astype(jnp.float16)


def build(sizes):
    ring = sizes[0] * 2

    strips = sizes[0] * sizes[1] * 4

    def along(value, step):
        def route(yh, x, c, yl):
            strip = ((yh * sizes[1] + x) * 2 + c) * 2 + yl + step
            if not 0 <= strip < strips:
                return None
            return (strip // 4 // sizes[1], strip // 4 % sizes[1], strip // 2 % 2, strip % 2)

        return exchange(value, ("yh", "x", "c", "yl"), (sizes[0], sizes[1], 2, 2), route)

    def across(value):
        return lax.ppermute(value, "yl", [(0, 1), (1, 0)])

    def local(tokens, proj_weight, feat_taps, inner_taps, grad_out):
        upper = lax.axis_index("yl")
        flag = upper.astype(jnp.int32).reshape(1)

        note = message(flag, grad_out, feat_taps, inner_taps)
        planes = proj_weight.transpose(1, 0, 2)
        rows, sent, note = lax.optimization_barrier((encode(tokens), planes, note))
        came = across(note)

        def beside(yh, c, yl):
            place = (yh * 2 + yl + (1 if c else ring - 1)) % ring
            return (place // 2, c, place % 2)

        theirs = exchange(sent, ("yh", "c", "yl"), (sizes[0], 2, 2), beside)
        gathered = lax.all_gather(rows, "z", axis=0, tiled=True)
        gathered, came = lax.optimization_barrier((gathered, came))
        gathered = gathered.astype(jnp.bfloat16)

        proj, head, tail = project(flag, gathered, grad_out, came, planes, theirs)
        prev = along(tail, 1)
        following = along(head, -1)
        kept, leaving, spread = mix(
            flag, proj, prev, following, grad_out, feat_taps, inner_taps, came, planes, theirs
        )
        arrived = across(leaving)
        summed = lax.psum_scatter(spread, "z", scatter_dimension=0, tiled=True)
        summed = lax.optimization_barrier(summed)
        depth = tokens.shape[1]
        grad_tokens = jnp.concatenate(
            [summed[:, :depth], summed[:FOLD, depth:].reshape(1, depth)], axis=0
        )
        grad_tokens, kept, arrived = lax.optimization_barrier((grad_tokens, kept, arrived))
        return (gather_halves(flag, kept, arrived), grad_tokens)

    return local


def solution(mesh):
    sizes = (4, 4, 2, 2, 12)
    grid = Mesh(mesh.devices.reshape(sizes), CTX + TP)
    in_specs = (
        P(CTX + TP, None),
        P(None, None, TP),
        P(None, None, TP),
        P(None, TP),
        P(CTX, TP),
    )
    out_specs = (P(CTX, TP), P(CTX + TP, None))
    return jax.shard_map(build(sizes), mesh=grid, in_specs=in_specs, out_specs=out_specs, check_vma=False)
```

```python
import jax
import jax.numpy as jnp
from jax import lax
from jax.experimental import pallas as pl
from jax.experimental.pallas import tpu as pltpu
from jax.sharding import Mesh
from jax.sharding import PartitionSpec as P

CTX = ("yh", "x", "c")
TP = ("yl", "z")
HALO = 8
TOP = 13.0
SHARD = 24
FOLD = 16


def exchange(value, axes, sizes, route):
    total = 1
    for size in sizes:
        total *= size
    pairs = []
    for source in range(total):
        coords, rest = [], source
        for size in reversed(sizes):
            coords.append(rest % size)
            rest //= size
        target = route(*reversed(coords))
        if target is None:
            continue
        flat = 0
        for place, size in zip(target, sizes):
            flat = flat * size + place
        pairs.append((source, flat))
    return lax.ppermute(value, axes, pairs)


def vmem():
    return pl.BlockSpec(memory_space=pltpu.MemorySpace.VMEM)


def smem():
    return pl.BlockSpec(memory_space=pltpu.MemorySpace.SMEM)


def hbm():
    return pl.BlockSpec(memory_space=pltpu.MemorySpace.HBM)


PARAMS = pltpu.CompilerParams(vmem_limit_bytes=24 * 1024 * 1024)


def slots(upper_ref, lanes):
    upper = upper_ref[0]
    return pl.multiple_of(upper * lanes, lanes), pl.multiple_of((1 - upper) * lanes, lanes)


def side_by_side(mine_ref, theirs_ref, part, cut):
    return jnp.concatenate([mine_ref[part, cut], theirs_ref[part, cut]], axis=1)


def message_kernel(upper_ref, grad_ref, feat_ref, inner_ref, o_ref):
    count = grad_ref.shape[0] // 2
    begin = pl.multiple_of((1 - upper_ref[0]) * count, 16)
    o_ref[:count] = grad_ref[pl.ds(begin, count)].astype(o_ref.dtype)
    for part in range(3):
        o_ref[count + 3 * part : count + 3 * part + 3] = feat_ref[part]
    o_ref[count + 9 :] = inner_ref[...]


def message(upper, grad, feat, inner):
    rows = grad.shape[0] // 2 + 9 + inner.shape[0]
    return pl.pallas_call(
        message_kernel,
        grid=(1,),
        in_specs=[smem()] + [pl.BlockSpec(v.shape, lambda i, n=v.ndim: (0,) * n) for v in (grad, feat, inner)],
        out_specs=pl.BlockSpec((rows, grad.shape[1]), lambda i: (0, 0)),
        out_shape=jax.ShapeDtypeStruct((rows, grad.shape[1]), jnp.float32),
        compiler_params=PARAMS,
        name="message",
    )(upper, grad, feat, inner)


def project_kernel(upper_ref, x_ref, grad_ref, came_ref, mine_ref, theirs_ref, o_ref, head_ref, tail_ref):
    parts, depth, lanes = mine_ref.shape
    count = x_ref.shape[0]
    own, other = slots(upper_ref, lanes)
    scale = jnp.exp2(x_ref[:, depth : depth + 1].astype(jnp.float32) - TOP)
    block = min(depth, 1024)
    for j in range(parts):
        total = None
        for begin in range(0, depth, block):
            cut = slice(begin, begin + block)
            piece = jnp.dot(
                x_ref[:, cut],
                side_by_side(mine_ref, theirs_ref, j, cut),
                preferred_element_type=jnp.float32,
            )
            total = piece if total is None else total + piece
        total = total * scale
        for place, half in ((own, total[:, :lanes]), (other, total[:, lanes:])):
            spot = pl.ds(place, lanes)
            o_ref[j, :, spot] = half.astype(o_ref.dtype)
            head_ref[j, :, spot] = half[:HALO].astype(head_ref.dtype)
            tail_ref[j, :, spot] = half[count - HALO :].astype(tail_ref.dtype)
    begin = pl.multiple_of(upper_ref[0] * count, 16)
    head_ref[parts, :, pl.ds(own, lanes)] = grad_ref[pl.ds(begin, count)][:HALO]
    head_ref[parts, :, pl.ds(other, lanes)] = came_ref[:HALO].astype(head_ref.dtype)


def project(upper, rows, grad, came, mine, theirs):
    parts, _, lanes = mine.shape
    count = rows.shape[0]
    return pl.pallas_call(
        project_kernel,
        in_specs=[smem()] + [vmem()] * 5,
        out_specs=[vmem()] * 3,
        out_shape=[
            jax.ShapeDtypeStruct((parts, count, 2 * lanes), jnp.bfloat16),
            jax.ShapeDtypeStruct((parts + 1, HALO, 2 * lanes), jnp.bfloat16),
            jax.ShapeDtypeStruct((parts, HALO, 2 * lanes), jnp.bfloat16),
        ],
        compiler_params=PARAMS,
        name="project",
    )(upper, rows, grad, came, mine, theirs)


def causal(series, taps):
    total = taps[0:1] * series
    for offset in range(1, taps.shape[0]):
        total = total + taps[offset : offset + 1] * pltpu.roll(series, offset, 0)
    return total


def adjoint(series, taps):
    total = taps[0:1] * series
    for offset in range(1, taps.shape[0]):
        total = total + taps[offset : offset + 1] * pltpu.roll(series, series.shape[0] - offset, 0)
    return total


def mix_kernel(
    upper_ref, proj_ref, prev_ref, next_ref, grad_ref, feat_ref, inner_ref, came_ref, mine_ref, theirs_ref,
    kept_ref, sent_ref, o_ref, back, extra, o_buf, sems,
):
    parts, depth, lanes = mine_ref.shape
    count = proj_ref.shape[1]
    last = HALO + count
    block = depth // 8
    own, other = slots(upper_ref, lanes)
    begin = pl.multiple_of(upper_ref[0] * count, 16)
    shards = count // SHARD
    body = SHARD - 1
    main = shards * body
    taps = came_ref[count:]
    sides = (
        (own, grad_ref[pl.ds(begin, count)], [feat_ref[part] for part in range(parts)], inner_ref[...], kept_ref),
        (other, came_ref[:count], [taps[3 * part : 3 * part + 3] for part in range(parts)], taps[9:], sent_ref),
    )
    for side, (place, here, feat, inner_taps, gated_ref) in enumerate(sides):
        spot = pl.ds(place, lanes)
        cut = slice(side * lanes, (side + 1) * lanes)

        def window(part):
            rows = [prev_ref[part, :, spot], proj_ref[part, :, spot], next_ref[part, :, spot]]
            return jnp.concatenate(rows, axis=0).astype(jnp.float32)

        query = causal(window(0), feat[0])
        key = causal(window(1), feat[1])
        value = causal(window(2), feat[2])
        inner = causal(key * value, inner_taps)
        gated_ref[...] = (query * inner)[HALO:last].astype(gated_ref.dtype)
        grad_next = next_ref[parts, :, spot].astype(jnp.float32)
        grad = jnp.concatenate([jnp.zeros_like(grad_next), here.astype(jnp.float32), grad_next], axis=0)
        mixed = adjoint(grad * query, inner_taps)
        for part, series in enumerate((grad * inner, mixed * value, mixed * key)):
            rows = adjoint(series, feat[part])[HALO:last]
            for k in range(shards):
                first = k * SHARD
                back[part, k * body : (k + 1) * body, cut] = rows[first : first + body]
                back[part, main + k : main + k + 1, cut] = rows[first + body : first + SHARD]
    left = [back[part].astype(jnp.bfloat16) for part in range(parts)]
    contract = (((1,), (1,)), ((), ()))
    extra[...] = jnp.zeros_like(extra)
    leaving = []
    wide = depth // FOLD
    for i in range(depth // block):
        cut = slice(i * block, (i + 1) * block)
        total = None
        for part in range(parts):
            piece = lax.dot_general(
                left[part],
                side_by_side(mine_ref, theirs_ref, part, cut),
                contract,
                preferred_element_type=jnp.float32,
            )
            total = piece if total is None else total + piece
        o_buf[:, cut] = total[:main].astype(o_buf.dtype)
        leaving.append(pltpu.make_async_copy(o_buf.at[:, cut], o_ref.at[:, cut], sems.at[i]))
        leaving[-1].start()
        for k in range(shards):
            for fold in range(block // wide):
                line = k * body + i * (block // wide) + fold
                extra[line : line + 1] = total[main + k : main + k + 1, fold * wide : (fold + 1) * wide]
    o_buf[:, depth:] = extra[...].astype(o_buf.dtype)
    leaving.append(pltpu.make_async_copy(o_buf.at[:, depth:], o_ref.at[:, depth:], sems.at[8]))
    leaving[-1].start()
    for copy in leaving:
        copy.wait()


def mix(upper, proj, prev, following, grad, feat, inner, came, mine, theirs):
    parts, depth, lanes = mine.shape
    count = proj.shape[1]
    half = jax.ShapeDtypeStruct((count, lanes), jnp.bfloat16)
    main = count // SHARD * (SHARD - 1)
    return pl.pallas_call(
        mix_kernel,
        in_specs=[smem()] + [vmem()] * 9,
        out_specs=[vmem(), vmem(), hbm()],
        out_shape=[half, half, pltpu.HBM((main, depth + depth // FOLD), jnp.bfloat16)],
        scratch_shapes=[
            pltpu.VMEM((parts, count, 2 * lanes), jnp.float32),
            pltpu.VMEM((main, depth // FOLD), jnp.float32),
            pltpu.VMEM((main, depth + depth // FOLD), jnp.bfloat16),
            pltpu.SemaphoreType.DMA((9,)),
        ],
        compiler_params=PARAMS,
        name="mix",
    )(upper, proj, prev, following, grad, feat, inner, came, mine, theirs)


def halves_kernel(upper_ref, kept_ref, arrived_ref, o_ref):
    count = kept_ref.shape[0]
    upper = upper_ref[0]
    o_ref[pl.ds(pl.multiple_of(upper * count, 16), count)] = kept_ref[...]
    o_ref[pl.ds(pl.multiple_of((1 - upper) * count, 16), count)] = arrived_ref[...]


def gather_halves(upper, kept, arrived):
    count, lanes = kept.shape
    return pl.pallas_call(
        halves_kernel,
        in_specs=[smem(), vmem(), vmem()],
        out_specs=vmem(),
        out_shape=jax.ShapeDtypeStruct((2 * count, lanes), kept.dtype),
        compiler_params=PARAMS,
        name="halves",
    )(upper, kept, arrived)


def encode(tokens):
    wide = tokens.astype(jnp.float32)
    peak = jnp.max(jnp.abs(wide), axis=1, keepdims=True)
    power = jnp.clip(jnp.floor(jnp.log2(jnp.maximum(peak, 1e-37))), -110.0, 110.0)
    scaled = wide * jnp.exp2(TOP - power)
    return jnp.concatenate(
        [scaled, jnp.broadcast_to(power, (tokens.shape[0], 128))], axis=1
    ).astype(jnp.float16)


def build(sizes):
    ring = sizes[0] * 2

    strips = sizes[0] * sizes[1] * 4

    def along(value, step):
        def route(yh, x, c, yl):
            strip = ((yh * sizes[1] + x) * 2 + c) * 2 + yl + step
            if not 0 <= strip < strips:
                return None
            return (strip // 4 // sizes[1], strip // 4 % sizes[1], strip // 2 % 2, strip % 2)

        return exchange(value, ("yh", "x", "c", "yl"), (sizes[0], sizes[1], 2, 2), route)

    def across(value):
        return lax.ppermute(value, "yl", [(0, 1), (1, 0)])

    def local(tokens, proj_weight, feat_taps, inner_taps, grad_out):
        upper = lax.axis_index("yl")
        flag = upper.astype(jnp.int32).reshape(1)

        note = message(flag, grad_out, feat_taps, inner_taps)
        planes = proj_weight.transpose(1, 0, 2)
        rows, sent, came = lax.optimization_barrier((encode(tokens), planes, across(note)))

        def beside(yh, c, yl):
            place = (yh * 2 + yl + (1 if c else ring - 1)) % ring
            return (place // 2, c, place % 2)

        theirs = exchange(sent, ("yh", "c", "yl"), (sizes[0], 2, 2), beside)
        gathered = lax.all_gather(rows, "z", axis=0, tiled=True)
        gathered, came = lax.optimization_barrier((gathered, came))
        gathered = gathered.astype(jnp.bfloat16)

        proj, head, tail = project(flag, gathered, grad_out, came, planes, theirs)
        prev = along(tail, 1)
        following = along(head, -1)
        kept, leaving, spread = mix(
            flag, proj, prev, following, grad_out, feat_taps, inner_taps, came, planes, theirs
        )
        arrived = across(leaving)
        summed = lax.psum_scatter(spread, "z", scatter_dimension=0, tiled=True)
        summed = lax.optimization_barrier(summed)
        depth = tokens.shape[1]
        grad_tokens = jnp.concatenate(
            [summed[:, :depth], summed[:FOLD, depth:].reshape(1, depth)], axis=0
        )
        return (gather_halves(flag, kept, arrived), grad_tokens)

    return local


def solution(mesh):
    sizes = (4, 4, 2, 2, 12)
    grid = Mesh(mesh.devices.reshape(sizes), CTX + TP)
    in_specs = (
        P(CTX + TP, None),
        P(None, None, TP),
        P(None, None, TP),
        P(None, TP),
        P(CTX, TP),
    )
    out_specs = (P(CTX, TP), P(CTX + TP, None))
    return jax.shard_map(build(sizes), mesh=grid, in_specs=in_specs, out_specs=out_specs, check_vma=False)
```

```python
import jax
import jax.numpy as jnp
from jax import lax
from jax.experimental import pallas as pl
from jax.experimental.pallas import tpu as pltpu
from jax.sharding import Mesh
from jax.sharding import PartitionSpec as P

CTX = ("yh", "x", "c")
TP = ("yl", "z")
HALO = 8
TOP = 13.0
SHARD = 24
FOLD = 16


def exchange(value, axes, sizes, route):
    total = 1
    for size in sizes:
        total *= size
    pairs = []
    for source in range(total):
        coords, rest = [], source
        for size in reversed(sizes):
            coords.append(rest % size)
            rest //= size
        target = route(*reversed(coords))
        if target is None:
            continue
        flat = 0
        for place, size in zip(target, sizes):
            flat = flat * size + place
        pairs.append((source, flat))
    return lax.ppermute(value, axes, pairs)


def vmem():
    return pl.BlockSpec(memory_space=pltpu.MemorySpace.VMEM)


def smem():
    return pl.BlockSpec(memory_space=pltpu.MemorySpace.SMEM)


def hbm():
    return pl.BlockSpec(memory_space=pltpu.MemorySpace.HBM)


PARAMS = pltpu.CompilerParams(vmem_limit_bytes=24 * 1024 * 1024)


def slots(upper_ref, lanes):
    upper = upper_ref[0]
    return pl.multiple_of(upper * lanes, lanes), pl.multiple_of((1 - upper) * lanes, lanes)


def bring(source, target, sems):
    copies = [pltpu.make_async_copy(source.at[j], target.at[j], sems.at[j]) for j in range(source.shape[0])]
    for copy in copies:
        copy.start()
    return copies


def side_by_side(mine_ref, theirs_ref, part, cut):
    return jnp.concatenate([mine_ref[part, cut], theirs_ref[part, cut]], axis=1)


def message_kernel(upper_ref, grad_ref, feat_ref, inner_ref, o_ref, grad_buf, feat_buf, inner_buf, sems):
    count = grad_buf.shape[0]
    begin = pl.multiple_of((1 - upper_ref[0]) * count, 16)
    copies = [
        pltpu.make_async_copy(grad_ref.at[pl.ds(begin, count)], grad_buf, sems.at[0]),
        pltpu.make_async_copy(feat_ref, feat_buf, sems.at[1]),
        pltpu.make_async_copy(inner_ref, inner_buf, sems.at[2]),
    ]
    for copy in copies:
        copy.start()
    for copy in copies:
        copy.wait()
    o_ref[:count] = grad_buf[...].astype(o_ref.dtype)
    for part in range(3):
        o_ref[count + 3 * part : count + 3 * part + 3] = feat_buf[part]
    o_ref[count + 9 :] = inner_buf[...]


def message(upper, grad, feat, inner):
    half = (grad.shape[0] // 2, grad.shape[1])
    return pl.pallas_call(
        message_kernel,
        in_specs=[smem()] + [hbm()] * 3,
        out_specs=vmem(),
        out_shape=jax.ShapeDtypeStruct((half[0] + 9 + inner.shape[0], half[1]), jnp.float32),
        scratch_shapes=[
            pltpu.VMEM(half, grad.dtype),
            pltpu.VMEM(feat.shape, feat.dtype),
            pltpu.VMEM(inner.shape, inner.dtype),
            pltpu.SemaphoreType.DMA((3,)),
        ],
        compiler_params=PARAMS,
        name="message",
    )(upper, *[in_hbm(value) for value in (grad, feat, inner)])


def in_hbm(value):
    return pltpu.with_memory_space_constraint(value, pltpu.MemorySpace.HBM)


def project_kernel(upper_ref, x_ref, grad_ref, came_ref, mine_hbm, theirs_ref, o_ref, head_ref, tail_ref, mine_ref, sems):
    parts, depth, lanes = mine_ref.shape
    count = x_ref.shape[0]
    own, other = slots(upper_ref, lanes)
    copies = bring(mine_hbm, mine_ref, sems)
    scale = jnp.exp2(x_ref[:, depth : depth + 1].astype(jnp.float32) - TOP)
    block = min(depth, 1024)
    for j in range(parts):
        total = None
        copies[j].wait()
        for begin in range(0, depth, block):
            cut = slice(begin, begin + block)
            piece = jnp.dot(
                x_ref[:, cut],
                side_by_side(mine_ref, theirs_ref, j, cut),
                preferred_element_type=jnp.float32,
            )
            total = piece if total is None else total + piece
        total = total * scale
        for place, half in ((own, total[:, :lanes]), (other, total[:, lanes:])):
            spot = pl.ds(place, lanes)
            o_ref[j, :, spot] = half.astype(o_ref.dtype)
            head_ref[j, :, spot] = half[:HALO].astype(head_ref.dtype)
            tail_ref[j, :, spot] = half[count - HALO :].astype(tail_ref.dtype)
    begin = pl.multiple_of(upper_ref[0] * count, 16)
    head_ref[parts, :, pl.ds(own, lanes)] = grad_ref[pl.ds(begin, count)][:HALO]
    head_ref[parts, :, pl.ds(other, lanes)] = came_ref[:HALO].astype(head_ref.dtype)


def project(upper, rows, grad, came, mine, theirs):
    parts, _, lanes = mine.shape
    count = rows.shape[0]
    return pl.pallas_call(
        project_kernel,
        in_specs=[smem()] + [vmem()] * 3 + [hbm(), vmem()],
        out_specs=[vmem()] * 3,
        out_shape=[
            jax.ShapeDtypeStruct((parts, count, 2 * lanes), jnp.bfloat16),
            jax.ShapeDtypeStruct((parts + 1, HALO, 2 * lanes), jnp.bfloat16),
            jax.ShapeDtypeStruct((parts, HALO, 2 * lanes), jnp.bfloat16),
        ],
        scratch_shapes=[pltpu.VMEM(mine.shape, mine.dtype), pltpu.SemaphoreType.DMA((parts,))],
        compiler_params=PARAMS,
        name="project",
    )(upper, rows, grad, came, in_hbm(mine), theirs)


def causal(series, taps):
    total = taps[0:1] * series
    for offset in range(1, taps.shape[0]):
        total = total + taps[offset : offset + 1] * pltpu.roll(series, offset, 0)
    return total


def adjoint(series, taps):
    total = taps[0:1] * series
    for offset in range(1, taps.shape[0]):
        total = total + taps[offset : offset + 1] * pltpu.roll(series, series.shape[0] - offset, 0)
    return total


def mix_kernel(
    upper_ref, proj_ref, prev_ref, next_ref, grad_ref, feat_ref, inner_ref, came_ref, mine_hbm, theirs_ref,
    kept_ref, sent_ref, o_ref, back, extra, o_buf, sems, mine_ref, mine_sems,
):
    parts, depth, lanes = mine_ref.shape
    count = proj_ref.shape[1]
    last = HALO + count
    block = depth // 8
    copies = bring(mine_hbm, mine_ref, mine_sems)
    own, other = slots(upper_ref, lanes)
    begin = pl.multiple_of(upper_ref[0] * count, 16)
    shards = count // SHARD
    body = SHARD - 1
    main = shards * body
    taps = came_ref[count:]
    sides = (
        (own, grad_ref[pl.ds(begin, count)], [feat_ref[part] for part in range(parts)], inner_ref[...], kept_ref),
        (other, came_ref[:count], [taps[3 * part : 3 * part + 3] for part in range(parts)], taps[9:], sent_ref),
    )
    for side, (place, here, feat, inner_taps, gated_ref) in enumerate(sides):
        spot = pl.ds(place, lanes)
        cut = slice(side * lanes, (side + 1) * lanes)

        def window(part):
            rows = [prev_ref[part, :, spot], proj_ref[part, :, spot], next_ref[part, :, spot]]
            return jnp.concatenate(rows, axis=0).astype(jnp.float32)

        query = causal(window(0), feat[0])
        key = causal(window(1), feat[1])
        value = causal(window(2), feat[2])
        inner = causal(key * value, inner_taps)
        gated_ref[...] = (query * inner)[HALO:last].astype(gated_ref.dtype)
        grad_next = next_ref[parts, :, spot].astype(jnp.float32)
        grad = jnp.concatenate([jnp.zeros_like(grad_next), here.astype(jnp.float32), grad_next], axis=0)
        mixed = adjoint(grad * query, inner_taps)
        for part, series in enumerate((grad * inner, mixed * value, mixed * key)):
            rows = adjoint(series, feat[part])[HALO:last]
            for k in range(shards):
                first = k * SHARD
                back[part, k * body : (k + 1) * body, cut] = rows[first : first + body]
                back[part, main + k : main + k + 1, cut] = rows[first + body : first + SHARD]
    for copy in copies:
        copy.wait()
    left = [back[part].astype(jnp.bfloat16) for part in range(parts)]
    contract = (((1,), (1,)), ((), ()))
    extra[...] = jnp.zeros_like(extra)
    leaving = []
    wide = depth // FOLD
    for i in range(depth // block):
        cut = slice(i * block, (i + 1) * block)
        total = None
        for part in range(parts):
            piece = lax.dot_general(
                left[part],
                side_by_side(mine_ref, theirs_ref, part, cut),
                contract,
                preferred_element_type=jnp.float32,
            )
            total = piece if total is None else total + piece
        o_buf[:, cut] = total[:main].astype(o_buf.dtype)
        leaving.append(pltpu.make_async_copy(o_buf.at[:, cut], o_ref.at[:, cut], sems.at[i]))
        leaving[-1].start()
        for k in range(shards):
            for fold in range(block // wide):
                line = k * body + i * (block // wide) + fold
                extra[line : line + 1] = total[main + k : main + k + 1, fold * wide : (fold + 1) * wide]
    o_buf[:, depth:] = extra[...].astype(o_buf.dtype)
    leaving.append(pltpu.make_async_copy(o_buf.at[:, depth:], o_ref.at[:, depth:], sems.at[8]))
    leaving[-1].start()
    for copy in leaving:
        copy.wait()


def mix(upper, proj, prev, following, grad, feat, inner, came, mine, theirs):
    parts, depth, lanes = mine.shape
    count = proj.shape[1]
    half = jax.ShapeDtypeStruct((count, lanes), jnp.bfloat16)
    main = count // SHARD * (SHARD - 1)
    return pl.pallas_call(
        mix_kernel,
        in_specs=[smem()] + [vmem()] * 7 + [hbm(), vmem()],
        out_specs=[vmem(), vmem(), hbm()],
        out_shape=[half, half, pltpu.HBM((main, depth + depth // FOLD), jnp.bfloat16)],
        scratch_shapes=[
            pltpu.VMEM((parts, count, 2 * lanes), jnp.float32),
            pltpu.VMEM((main, depth // FOLD), jnp.float32),
            pltpu.VMEM((main, depth + depth // FOLD), jnp.bfloat16),
            pltpu.SemaphoreType.DMA((9,)),
            pltpu.VMEM(mine.shape, mine.dtype),
            pltpu.SemaphoreType.DMA((parts,)),
        ],
        compiler_params=PARAMS,
        name="mix",
    )(upper, proj, prev, following, grad, feat, inner, came, in_hbm(mine), theirs)


def halves_kernel(upper_ref, kept_ref, arrived_ref, o_ref):
    count = kept_ref.shape[0]
    upper = upper_ref[0]
    o_ref[pl.ds(pl.multiple_of(upper * count, 16), count)] = kept_ref[...]
    o_ref[pl.ds(pl.multiple_of((1 - upper) * count, 16), count)] = arrived_ref[...]


def gather_halves(upper, kept, arrived):
    count, lanes = kept.shape
    return pl.pallas_call(
        halves_kernel,
        in_specs=[smem(), vmem(), vmem()],
        out_specs=vmem(),
        out_shape=jax.ShapeDtypeStruct((2 * count, lanes), kept.dtype),
        compiler_params=PARAMS,
        name="halves",
    )(upper, kept, arrived)


def encode(tokens):
    wide = tokens.astype(jnp.float32)
    peak = jnp.max(jnp.abs(wide), axis=1, keepdims=True)
    power = jnp.clip(jnp.floor(jnp.log2(jnp.maximum(peak, 1e-37))), -110.0, 110.0)
    scaled = wide * jnp.exp2(TOP - power)
    return jnp.concatenate(
        [scaled, jnp.broadcast_to(power, (tokens.shape[0], 128))], axis=1
    ).astype(jnp.float16)


def build(sizes):
    ring = sizes[0] * 2

    strips = sizes[0] * sizes[1] * 4

    def along(value, step):
        def route(yh, x, c, yl):
            strip = ((yh * sizes[1] + x) * 2 + c) * 2 + yl + step
            if not 0 <= strip < strips:
                return None
            return (strip // 4 // sizes[1], strip // 4 % sizes[1], strip // 2 % 2, strip % 2)

        return exchange(value, ("yh", "x", "c", "yl"), (sizes[0], sizes[1], 2, 2), route)

    def across(value):
        return lax.ppermute(value, "yl", [(0, 1), (1, 0)])

    def local(tokens, proj_weight, feat_taps, inner_taps, grad_out):
        upper = lax.axis_index("yl")
        flag = upper.astype(jnp.int32).reshape(1)

        note = message(flag, grad_out, feat_taps, inner_taps)
        planes = proj_weight.transpose(1, 0, 2)
        rows, sent, came = lax.optimization_barrier((encode(tokens), planes, across(note)))

        def beside(yh, c, yl):
            place = (yh * 2 + yl + (1 if c else ring - 1)) % ring
            return (place // 2, c, place % 2)

        theirs = exchange(sent, ("yh", "c", "yl"), (sizes[0], 2, 2), beside)
        gathered = lax.all_gather(rows, "z", axis=0, tiled=True)
        gathered, came = lax.optimization_barrier((gathered, came))
        gathered = gathered.astype(jnp.bfloat16)

        proj, head, tail = project(flag, gathered, grad_out, came, planes, theirs)
        prev = along(tail, 1)
        following = along(head, -1)
        kept, leaving, spread = mix(
            flag, proj, prev, following, grad_out, feat_taps, inner_taps, came, planes, theirs
        )
        arrived = across(leaving)
        summed = lax.psum_scatter(spread, "z", scatter_dimension=0, tiled=True)
        summed = lax.optimization_barrier(summed)
        depth = tokens.shape[1]
        grad_tokens = jnp.concatenate(
            [summed[:, :depth], summed[:FOLD, depth:].reshape(1, depth)], axis=0
        )
        return (gather_halves(flag, kept, arrived), grad_tokens)

    return local


def solution(mesh):
    sizes = (4, 4, 2, 2, 12)
    grid = Mesh(mesh.devices.reshape(sizes), CTX + TP)
    in_specs = (
        P(CTX + TP, None),
        P(None, None, TP),
        P(None, None, TP),
        P(None, TP),
        P(CTX, TP),
    )
    out_specs = (P(CTX, TP), P(CTX + TP, None))
    return jax.shard_map(build(sizes), mesh=grid, in_specs=in_specs, out_specs=out_specs, check_vma=False)
```

```python
import jax
import jax.numpy as jnp
from jax import lax
from jax.experimental import pallas as pl
from jax.experimental.pallas import tpu as pltpu
from jax.sharding import Mesh
from jax.sharding import PartitionSpec as P

CTX = ("yh", "x", "c")
TP = ("yl", "z")
HALO = 8
TOP = 13.0
SHARD = 24
FOLD = 16


def exchange(value, axes, sizes, route):
    total = 1
    for size in sizes:
        total *= size
    pairs = []
    for source in range(total):
        coords, rest = [], source
        for size in reversed(sizes):
            coords.append(rest % size)
            rest //= size
        target = route(*reversed(coords))
        if target is None:
            continue
        flat = 0
        for place, size in zip(target, sizes):
            flat = flat * size + place
        pairs.append((source, flat))
    return lax.ppermute(value, axes, pairs)


def vmem():
    return pl.BlockSpec(memory_space=pltpu.MemorySpace.VMEM)


def smem():
    return pl.BlockSpec(memory_space=pltpu.MemorySpace.SMEM)


def hbm():
    return pl.BlockSpec(memory_space=pltpu.MemorySpace.HBM)


PARAMS = pltpu.CompilerParams(vmem_limit_bytes=24 * 1024 * 1024)


def slots(upper_ref, lanes):
    upper = upper_ref[0]
    return pl.multiple_of(upper * lanes, lanes), pl.multiple_of((1 - upper) * lanes, lanes)


def side_by_side(mine_ref, theirs_ref, part, cut):
    return jnp.concatenate([mine_ref[part, cut], theirs_ref[part, cut]], axis=1)


def message_kernel(upper_ref, grad_ref, feat_ref, inner_ref, o_ref, grad_buf, feat_buf, inner_buf, sems):
    count = grad_buf.shape[0]
    begin = pl.multiple_of((1 - upper_ref[0]) * count, 16)
    copies = [
        pltpu.make_async_copy(grad_ref.at[pl.ds(begin, count)], grad_buf, sems.at[0]),
        pltpu.make_async_copy(feat_ref, feat_buf, sems.at[1]),
        pltpu.make_async_copy(inner_ref, inner_buf, sems.at[2]),
    ]
    for copy in copies:
        copy.start()
    for copy in copies:
        copy.wait()
    o_ref[:count] = grad_buf[...].astype(o_ref.dtype)
    for part in range(3):
        o_ref[count + 3 * part : count + 3 * part + 3] = feat_buf[part]
    o_ref[count + 9 :] = inner_buf[...]


def message(upper, grad, feat, inner):
    half = (grad.shape[0] // 2, grad.shape[1])
    return pl.pallas_call(
        message_kernel,
        in_specs=[smem()] + [hbm()] * 3,
        out_specs=vmem(),
        out_shape=jax.ShapeDtypeStruct((half[0] + 9 + inner.shape[0], half[1]), jnp.float32),
        scratch_shapes=[
            pltpu.VMEM(half, grad.dtype),
            pltpu.VMEM(feat.shape, feat.dtype),
            pltpu.VMEM(inner.shape, inner.dtype),
            pltpu.SemaphoreType.DMA((3,)),
        ],
        compiler_params=PARAMS,
        name="message",
    )(upper, *[in_hbm(value) for value in (grad, feat, inner)])


def in_hbm(value):
    return pltpu.with_memory_space_constraint(value, pltpu.MemorySpace.HBM)


def project_kernel(upper_ref, x_ref, grad_ref, came_ref, mine_ref, theirs_ref, o_ref, head_ref, tail_ref):
    parts, depth, lanes = mine_ref.shape
    count = x_ref.shape[0]
    own, other = slots(upper_ref, lanes)
    scale = jnp.exp2(x_ref[:, depth : depth + 1].astype(jnp.float32) - TOP)
    block = min(depth, 1024)
    for j in range(parts):
        total = None
        for begin in range(0, depth, block):
            cut = slice(begin, begin + block)
            piece = jnp.dot(
                x_ref[:, cut],
                side_by_side(mine_ref, theirs_ref, j, cut),
                preferred_element_type=jnp.float32,
            )
            total = piece if total is None else total + piece
        total = total * scale
        for place, half in ((own, total[:, :lanes]), (other, total[:, lanes:])):
            spot = pl.ds(place, lanes)
            o_ref[j, :, spot] = half.astype(o_ref.dtype)
            head_ref[j, :, spot] = half[:HALO].astype(head_ref.dtype)
            tail_ref[j, :, spot] = half[count - HALO :].astype(tail_ref.dtype)
    begin = pl.multiple_of(upper_ref[0] * count, 16)
    head_ref[parts, :, pl.ds(own, lanes)] = grad_ref[pl.ds(begin, count)][:HALO]
    head_ref[parts, :, pl.ds(other, lanes)] = came_ref[:HALO].astype(head_ref.dtype)


def project(upper, rows, grad, came, mine, theirs):
    parts, _, lanes = mine.shape
    count = rows.shape[0]
    return pl.pallas_call(
        project_kernel,
        in_specs=[smem()] + [vmem()] * 5,
        out_specs=[vmem()] * 3,
        out_shape=[
            jax.ShapeDtypeStruct((parts, count, 2 * lanes), jnp.bfloat16),
            jax.ShapeDtypeStruct((parts + 1, HALO, 2 * lanes), jnp.bfloat16),
            jax.ShapeDtypeStruct((parts, HALO, 2 * lanes), jnp.bfloat16),
        ],
        compiler_params=PARAMS,
        name="project",
    )(upper, rows, grad, came, mine, theirs)


def causal(series, taps):
    total = taps[0:1] * series
    for offset in range(1, taps.shape[0]):
        total = total + taps[offset : offset + 1] * pltpu.roll(series, offset, 0)
    return total


def adjoint(series, taps):
    total = taps[0:1] * series
    for offset in range(1, taps.shape[0]):
        total = total + taps[offset : offset + 1] * pltpu.roll(series, series.shape[0] - offset, 0)
    return total


def mix_kernel(
    upper_ref, proj_ref, prev_ref, next_ref, grad_ref, feat_ref, inner_ref, came_ref, mine_ref, theirs_ref,
    kept_ref, sent_ref, o_ref, back, extra, o_buf, sems,
):
    parts, depth, lanes = mine_ref.shape
    count = proj_ref.shape[1]
    last = HALO + count
    block = depth // 8
    own, other = slots(upper_ref, lanes)
    begin = pl.multiple_of(upper_ref[0] * count, 16)
    shards = count // SHARD
    body = SHARD - 1
    main = shards * body
    taps = came_ref[count:]
    sides = (
        (own, grad_ref[pl.ds(begin, count)], [feat_ref[part] for part in range(parts)], inner_ref[...], kept_ref),
        (other, came_ref[:count], [taps[3 * part : 3 * part + 3] for part in range(parts)], taps[9:], sent_ref),
    )
    for side, (place, here, feat, inner_taps, gated_ref) in enumerate(sides):
        spot = pl.ds(place, lanes)
        cut = slice(side * lanes, (side + 1) * lanes)

        def window(part):
            rows = [prev_ref[part, :, spot], proj_ref[part, :, spot], next_ref[part, :, spot]]
            return jnp.concatenate(rows, axis=0).astype(jnp.float32)

        query = causal(window(0), feat[0])
        key = causal(window(1), feat[1])
        value = causal(window(2), feat[2])
        inner = causal(key * value, inner_taps)
        gated_ref[...] = (query * inner)[HALO:last].astype(gated_ref.dtype)
        grad_next = next_ref[parts, :, spot].astype(jnp.float32)
        grad = jnp.concatenate([jnp.zeros_like(grad_next), here.astype(jnp.float32), grad_next], axis=0)
        mixed = adjoint(grad * query, inner_taps)
        for part, series in enumerate((grad * inner, mixed * value, mixed * key)):
            rows = adjoint(series, feat[part])[HALO:last]
            for k in range(shards):
                first = k * SHARD
                back[part, k * body : (k + 1) * body, cut] = rows[first : first + body]
                back[part, main + k : main + k + 1, cut] = rows[first + body : first + SHARD]
    left = [back[part].astype(jnp.bfloat16) for part in range(parts)]
    contract = (((1,), (1,)), ((), ()))
    extra[...] = jnp.zeros_like(extra)
    leaving = []
    wide = depth // FOLD
    for i in range(depth // block):
        cut = slice(i * block, (i + 1) * block)
        total = None
        for part in range(parts):
            piece = lax.dot_general(
                left[part],
                side_by_side(mine_ref, theirs_ref, part, cut),
                contract,
                preferred_element_type=jnp.float32,
            )
            total = piece if total is None else total + piece
        o_buf[:, cut] = total[:main].astype(o_buf.dtype)
        leaving.append(pltpu.make_async_copy(o_buf.at[:, cut], o_ref.at[:, cut], sems.at[i]))
        leaving[-1].start()
        for k in range(shards):
            for fold in range(block // wide):
                line = k * body + i * (block // wide) + fold
                extra[line : line + 1] = total[main + k : main + k + 1, fold * wide : (fold + 1) * wide]
    o_buf[:, depth:] = extra[...].astype(o_buf.dtype)
    leaving.append(pltpu.make_async_copy(o_buf.at[:, depth:], o_ref.at[:, depth:], sems.at[8]))
    leaving[-1].start()
    for copy in leaving:
        copy.wait()


def mix(upper, proj, prev, following, grad, feat, inner, came, mine, theirs):
    parts, depth, lanes = mine.shape
    count = proj.shape[1]
    half = jax.ShapeDtypeStruct((count, lanes), jnp.bfloat16)
    main = count // SHARD * (SHARD - 1)
    return pl.pallas_call(
        mix_kernel,
        in_specs=[smem()] + [vmem()] * 9,
        out_specs=[vmem(), vmem(), hbm()],
        out_shape=[half, half, pltpu.HBM((main, depth + depth // FOLD), jnp.bfloat16)],
        scratch_shapes=[
            pltpu.VMEM((parts, count, 2 * lanes), jnp.float32),
            pltpu.VMEM((main, depth // FOLD), jnp.float32),
            pltpu.VMEM((main, depth + depth // FOLD), jnp.bfloat16),
            pltpu.SemaphoreType.DMA((9,)),
        ],
        compiler_params=PARAMS,
        name="mix",
    )(upper, proj, prev, following, grad, feat, inner, came, mine, theirs)


def halves_kernel(upper_ref, kept_ref, arrived_ref, o_ref):
    count = kept_ref.shape[0]
    upper = upper_ref[0]
    o_ref[pl.ds(pl.multiple_of(upper * count, 16), count)] = kept_ref[...]
    o_ref[pl.ds(pl.multiple_of((1 - upper) * count, 16), count)] = arrived_ref[...]


def gather_halves(upper, kept, arrived):
    count, lanes = kept.shape
    return pl.pallas_call(
        halves_kernel,
        in_specs=[smem(), vmem(), vmem()],
        out_specs=vmem(),
        out_shape=jax.ShapeDtypeStruct((2 * count, lanes), kept.dtype),
        compiler_params=PARAMS,
        name="halves",
    )(upper, kept, arrived)


def encode(tokens):
    wide = tokens.astype(jnp.float32)
    peak = jnp.max(jnp.abs(wide), axis=1, keepdims=True)
    power = jnp.clip(jnp.floor(jnp.log2(jnp.maximum(peak, 1e-37))), -110.0, 110.0)
    scaled = wide * jnp.exp2(TOP - power)
    return jnp.concatenate(
        [scaled, jnp.broadcast_to(power, (tokens.shape[0], 128))], axis=1
    ).astype(jnp.float16)


def build(sizes):
    ring = sizes[0] * 2

    strips = sizes[0] * sizes[1] * 4

    def along(value, step):
        def route(yh, x, c, yl):
            strip = ((yh * sizes[1] + x) * 2 + c) * 2 + yl + step
            if not 0 <= strip < strips:
                return None
            return (strip // 4 // sizes[1], strip // 4 % sizes[1], strip // 2 % 2, strip % 2)

        return exchange(value, ("yh", "x", "c", "yl"), (sizes[0], sizes[1], 2, 2), route)

    def across(value):
        return lax.ppermute(value, "yl", [(0, 1), (1, 0)])

    def local(tokens, proj_weight, feat_taps, inner_taps, grad_out):
        upper = lax.axis_index("yl")
        flag = upper.astype(jnp.int32).reshape(1)

        note = message(flag, grad_out, feat_taps, inner_taps)
        planes = proj_weight.transpose(1, 0, 2)
        rows, sent, came = lax.optimization_barrier((encode(tokens), planes, across(note)))

        def beside(yh, c, yl):
            place = (yh * 2 + yl + (1 if c else ring - 1)) % ring
            return (place // 2, c, place % 2)

        theirs = exchange(sent, ("yh", "c", "yl"), (sizes[0], 2, 2), beside)
        gathered = lax.all_gather(rows, "z", axis=0, tiled=True)
        gathered, came = lax.optimization_barrier((gathered, came))
        gathered = gathered.astype(jnp.bfloat16)

        proj, head, tail = project(flag, gathered, grad_out, came, planes, theirs)
        prev = along(tail, 1)
        following = along(head, -1)
        kept, leaving, spread = mix(
            flag, proj, prev, following, grad_out, feat_taps, inner_taps, came, planes, theirs
        )
        arrived = across(leaving)
        summed = lax.psum_scatter(spread, "z", scatter_dimension=0, tiled=True)
        summed = lax.optimization_barrier(summed)
        depth = tokens.shape[1]
        grad_tokens = jnp.concatenate(
            [summed[:, :depth], summed[:FOLD, depth:].reshape(1, depth)], axis=0
        )
        return (gather_halves(flag, kept, arrived), grad_tokens)

    return local


def solution(mesh):
    sizes = (4, 4, 2, 2, 12)
    grid = Mesh(mesh.devices.reshape(sizes), CTX + TP)
    in_specs = (
        P(CTX + TP, None),
        P(None, None, TP),
        P(None, None, TP),
        P(None, TP),
        P(CTX, TP),
    )
    out_specs = (P(CTX, TP), P(CTX + TP, None))
    return jax.shard_map(build(sizes), mesh=grid, in_specs=in_specs, out_specs=out_specs, check_vma=False)
```
